512 devices in a mesh: rows: 128 (over z, x, y_hi, core), chan: 4 (over y_lo).
Axes of the slice: x: 4, y: 8 (y_hi: 2, y_lo: 4; y = y_hi * 4 + y_lo), z: 8, core: 2. Of those that a mesh axis runs over, the one named last changes fastest.
Arguments:
- za: bfloat16 [256, 48, 1024], P('rows', 'chan'), may hold values from -6 to 6
- zb: bfloat16 [256, 48, 1024], P('rows', 'chan'), may hold values from -6 to 6
- w_in: bfloat16 [3, 3, 48, 512], P(None, None, None, 'chan'), may hold values from -0.3125 to 0.3125
- b_in: float32 [512], P('chan'), may hold values from -3 to 3
- w_out: bfloat16 [3, 3, 512, 2, 48], P(None, None, 'chan'), may hold values from -0.09375 to 0.09375
- b_out: float32 [2, 48], replicated, may hold values from -3 to 3
- unmix: float32 [96, 96], replicated, may hold values from -0.625 to 0.625
- kern: float32 [3, 3, 96], replicated, may hold values from -1.4 to 1.4, as said below
Outputs:
- sample: float32 [256, 96, 1024], P('rows', 'chan')
The draws below stay inside these ranges and needn't reach their ends.
Inputs may be any that keep to these rules, and one draw needn't show every extreme that they name: `kern`: for every channel the centre entry is positive and the eight other entries are negative with magnitudes summing to less than the centre.
All inputs are finite; a program needn't handle non-finite values.
Results may differ from the reference program's by a relative error of at most 0.0015.
Values may be sent and summed in bfloat16 or wider, within the bound.
A program may use at most 64 MiB of HBM per device.

```python
import math
import jax
import jax.numpy as jnp
from jax import lax

C = 96
HID = 512
COLS = 1024
ROWS = 256


def draw_kern(key, part):
    key_pull, key_damp, key_gain = jax.random.split(key, 3)
    pulling = jax.random.uniform(key_pull, (9, C), jnp.float32, 0.2, 1.0)
    damping = jnp.exp(jax.random.uniform(key_damp, (C,), jnp.float32, math.log(0.02), math.log(0.3)))
    stencil_gain = jax.random.uniform(key_gain, (C,), jnp.float32, 0.7, 1.4)
    centre = (jnp.arange(9) == 4)[:, None]
    pulling = jnp.where(centre, 0.0, pulling)
    pulling = pulling * ((1.0 - damping) / jnp.sum(pulling, axis=0))[None, :]
    stencil = stencil_gain[None, :] * (centre.astype(jnp.float32) - pulling)
    return stencil.reshape(3, 3, C)


def steps_of(key, dims, pieces, low, high):
    def one(position, shards_of):
        draws = jax.random.uniform(jax.random.fold_in(jax.random.fold_in(key, 6), position), (shards_of,), jnp.float32, low / len(pieces), high / len(pieces))
        return jnp.repeat(jnp.exp(draws), dims[position] // shards_of).reshape((-1,) + (1,) * (len(dims) - position - 1))

    level = one(*pieces[0])
    for cut in pieces[1:]:
        level = level * one(*cut)
    return level


def gaussian(rng, dims, deviation, reach, pieces=(), kind=jnp.bfloat16):
    entries = jax.random.normal(rng, dims, jnp.float32) * deviation
    if len(pieces) > 0:
        entries = steps_of(rng, dims, pieces, -0.22, 0.18) * entries
    return jnp.clip(entries, min=-reach, max=reach).astype(kind)


def setup_inputs(seed: int = 0) -> dict:
    arg_keys = jax.random.split(jax.random.key(seed), 9)
    return {
        "za": gaussian(arg_keys[0], (ROWS, C // 2, COLS), 1.0, 6.0, ((0, 128), (1, 4))),
        "zb": gaussian(arg_keys[1], (ROWS, C // 2, COLS), 1.0, 6.0, ((0, 128), (1, 4))),
        "w_in": gaussian(arg_keys[2], (3, 3, C // 2, HID), (9 * C // 2) ** -0.5, 0.3125, ((3, 4),)),
        "b_in": gaussian(arg_keys[3], (HID,), 0.5, 3.0, ((0, 4),), jnp.float32),
        "w_out": gaussian(arg_keys[4], (3, 3, HID, 2, C // 2), (9 * HID) ** -0.5, 0.09375, ((2, 4),)),
        "b_out": gaussian(arg_keys[5], (2, C // 2), 0.5, 3.0, (), jnp.float32),
        "unmix": gaussian(arg_keys[6], (C, C), C ** -0.5, 0.625, (), jnp.float32),
        "kern": draw_kern(jax.random.fold_in(arg_keys[8], 71), 0),
    }


full_turn = 2.0 * math.pi


def conv_rows(source, weight):
    rows_out = source.shape[0] - 2
    width = source.shape[2]
    padded = jnp.pad(source.astype(jnp.float32), ((0, 0), (0, 0), (1, 1)))
    total = jnp.zeros((rows_out, weight.shape[3], width), jnp.float32)
    for row_off in range(3):
        for col_off in range(3):
            piece = padded[row_off:row_off + rows_out, :, col_off:col_off + width]
            total = total + jnp.einsum('rcw,co->row', piece, weight[row_off, col_off].astype(jnp.float32))
    return total


def stencil_spectrum(kern, freq_rows, height, freq_cols, width):
    shape = (freq_rows.shape[0], kern.shape[2], freq_cols.shape[0])
    real_part = jnp.zeros(shape, jnp.float32)
    imag_part = jnp.zeros(shape, jnp.float32)
    for row_off in range(3):
        for col_off in range(3):
            phase_rows = ((freq_rows * (row_off - 1)) % height).astype(jnp.float32) * (full_turn / height)
            phase_cols = ((freq_cols * (col_off - 1)) % width).astype(jnp.float32) * (full_turn / width)
            phase = phase_rows[:, None, None] + phase_cols[None, None, :]
            weight = kern[row_off, col_off][None, :, None]
            real_part = real_part + weight * jnp.cos(phase)
            imag_part = imag_part + weight * jnp.sin(phase)
    return real_part, imag_part


def reference(za, zb, w_in, b_in, w_out, b_out, unmix, kern):
    height, half, width = za.shape
    chans = 2 * half
    hidden_units = w_in.shape[3]
    block_len = math.gcd(height, 16)
    block_count = height // block_len
    za_pad = jnp.pad(za, ((2, 2), (0, 0), (0, 0)))
    w_flat = w_out.reshape(3, 3, hidden_units, chans)
    bias_out = b_out.reshape(chans)

    def coupling_block(block_idx):
        start = block_idx * block_len
        piece = lax.dynamic_slice_in_dim(za_pad, start, block_len + 4, 0)
        hidden = jax.nn.relu(conv_rows(piece, w_in) + b_in[None, :, None])
        global_rows = start - 1 + jnp.arange(block_len + 2, dtype=jnp.int32)
        inside = (global_rows >= 0) & (global_rows < height)
        hidden = jnp.where(inside[:, None, None], hidden, 0.0).astype(jnp.bfloat16)
        raw = conv_rows(hidden, w_flat) + bias_out[None, :, None]
        latent = lax.dynamic_slice_in_dim(zb, start, block_len, 0).astype(jnp.float32)
        return (latent - raw[:, half:]) * jnp.exp(-jnp.tanh(raw[:, :half]))

    coupled = lax.map(coupling_block, jnp.arange(block_count, dtype=jnp.int32))
    coupled = coupled.reshape(height, half, width)
    joined = jnp.concatenate([za.astype(jnp.float32), coupled], axis=1)
    mixed = jnp.einsum('oc,rcw->row', unmix, joined, precision=lax.Precision.HIGHEST)
    spectrum = jnp.fft.fft2(mixed, axes=(0, 2))
    symbol_real, symbol_imag = stencil_spectrum(kern, jnp.arange(height, dtype=jnp.int32), height, jnp.arange(width, dtype=jnp.int32), width)
    solved = spectrum / lax.complex(symbol_real, symbol_imag)
    return jnp.real(jnp.fft.ifft2(solved, axes=(0, 2))).astype(jnp.float32)
```

```python
import math

import jax
import jax.numpy as jnp
import numpy as np
from jax import lax
from jax.experimental import pallas as pl
from jax.experimental.pallas import tpu as pltpu
from jax.sharding import PartitionSpec as P

full_turn = 2.0 * math.pi
vmem = pl.BlockSpec(memory_space=pltpu.VMEM)
mesh_ids = pl.DeviceIdType.MESH


def swap_kernel(axis, count, x_ref, out_ref, send_sem, recv_sem, own_sem):
    me_row = lax.axis_index("rows")
    me_chan = lax.axis_index("chan")
    me = me_row if axis == "rows" else me_chan

    def place(peer):
        return (peer, me_chan) if axis == "rows" else (me_row, peer)

    barrier = pltpu.get_barrier_semaphore()

    def greet(step, carry):
        pl.semaphore_signal(
            barrier, inc=1, device_id=place(lax.rem(me + step, count)), device_id_type=mesh_ids
        )
        return carry

    lax.fori_loop(1, count, greet, 0)
    own = pltpu.make_async_copy(x_ref.at[me], out_ref.at[me], own_sem)
    own.start()
    pl.semaphore_wait(barrier, count - 1)

    def copy(step):
        peer = lax.rem(me + step, count)
        return pltpu.make_async_remote_copy(
            src_ref=x_ref.at[peer],
            dst_ref=out_ref.at[me],
            send_sem=send_sem.at[step],
            recv_sem=recv_sem.at[step],
            device_id=place(peer),
            device_id_type=mesh_ids,
        )

    def start(step, carry):
        copy(step).start()
        return carry

    def finish(step, carry):
        copy(step).wait()
        return carry

    lax.fori_loop(1, count, start, 0)
    own.wait()
    lax.fori_loop(1, count, finish, 0)


def swap(x, axis, ident):
    count = x.shape[0]

    def kernel(*refs):
        swap_kernel(axis, count, *refs)

    return pl.pallas_call(
        kernel,
        out_shape=jax.ShapeDtypeStruct(x.shape, x.dtype),
        in_specs=[vmem],
        out_specs=vmem,
        scratch_shapes=[
            pltpu.SemaphoreType.DMA((count,)),
            pltpu.SemaphoreType.DMA((count,)),
            pltpu.SemaphoreType.DMA,
        ],
        compiler_params=pltpu.CompilerParams(collective_id=ident, has_side_effects=True),
        name="swap_" + axis + str(ident),
    )(x)


def gather_kernel(rows, chans, za_ref, zb_ref, out_ref, zb_out, sems_a, sems_b, own_sem):
    me_row = lax.axis_index("rows")
    me_chan = lax.axis_index("chan")
    barrier = pltpu.get_barrier_semaphore()
    peers = [(dr, dc) for dr in (0, 1, 2) for dc in range(chans) if (dr, dc) != (1, 0)]

    def place(dr, dc):
        return (lax.rem(me_row + dr + rows - 1, rows), lax.rem(me_chan + dc, chans))

    for dr, dc in peers:
        pl.semaphore_signal(barrier, inc=1, device_id=place(dr, dc), device_id_type=mesh_ids)
    own = pltpu.make_async_copy(za_ref, out_ref.at[1, me_chan], own_sem.at[0])
    own.start()
    own_b = pltpu.make_async_copy(zb_ref.at[me_chan], zb_out.at[me_chan], own_sem.at[1])
    own_b.start()
    pl.semaphore_wait(barrier, len(peers))
    copies = []
    for idx, (dr, dc) in enumerate(peers):
        copies.append(
            pltpu.make_async_remote_copy(
                src_ref=za_ref,
                dst_ref=out_ref.at[2 - dr, me_chan],
                send_sem=sems_a.at[0, idx],
                recv_sem=sems_a.at[1, idx],
                device_id=place(dr, dc),
                device_id_type=mesh_ids,
            )
        )
    for dc in range(1, chans):
        peer = lax.rem(me_chan + dc, chans)
        copies.append(
            pltpu.make_async_remote_copy(
                src_ref=zb_ref.at[peer],
                dst_ref=zb_out.at[me_chan],
                send_sem=sems_b.at[0, dc],
                recv_sem=sems_b.at[1, dc],
                device_id=(me_row, peer),
                device_id_type=mesh_ids,
            )
        )
    for one in copies:
        one.start()
    own.wait()
    own_b.wait()
    for one in copies:
        one.wait()


def gather(za, zb_cols, rows, chans):
    def kernel(*refs):
        gather_kernel(rows, chans, *refs)

    return pl.pallas_call(
        kernel,
        out_shape=(
            jax.ShapeDtypeStruct((3, chans) + za.shape, za.dtype),
            jax.ShapeDtypeStruct(zb_cols.shape, zb_cols.dtype),
        ),
        in_specs=[vmem, vmem],
        out_specs=(vmem, vmem),
        scratch_shapes=[
            pltpu.SemaphoreType.DMA((2, 3 * chans)),
            pltpu.SemaphoreType.DMA((2, chans)),
            pltpu.SemaphoreType.DMA((2,)),
        ],
        compiler_params=pltpu.CompilerParams(collective_id=0, has_side_effects=True),
        name="gather_latents",
    )(za, zb_cols)


def conv_rows(source, weight):
    rows_out = source.shape[0] - 2
    width = source.shape[2]
    padded = jnp.pad(source, ((0, 0), (0, 0), (1, 1)))
    pieces = [
        padded[row_off : row_off + rows_out, :, col_off : col_off + width]
        for row_off in range(3)
        for col_off in range(3)
    ]
    stacked = jnp.stack(pieces, axis=1)
    taps = weight.reshape(9, weight.shape[2], weight.shape[3])
    return jnp.einsum("rkcw,kco->row", stacked, taps, preferred_element_type=jnp.float32)


def halves(values):
    high = lax.reduce_precision(values, 8, 7)
    return high.astype(jnp.bfloat16), (values - high).astype(jnp.bfloat16)


def column_tables(width, group):
    pos = np.arange(width)
    part = pos // group % 2
    slot = pos // (2 * group) * group + pos % group
    first = slot == 0
    freq = np.where(first & (part == 1), width // 2, slot)
    shift = np.where(first, 0, part) * (math.pi / 2)
    fine = 32
    outer = (np.arange(width // fine) * fine)[:, None] * freq[None, :] % width * (full_turn / width)
    inner = np.arange(fine)[:, None] * freq[None, :] % width * (full_turn / width) + shift[None, :]
    consts = [f(a).astype(np.float32) for a in (outer, inner) for f in (np.cos, np.sin)]
    cos_o, sin_o, cos_i, sin_i = lax.optimization_barrier(tuple(jnp.asarray(c) for c in consts))
    table = cos_o[:, None, :] * cos_i[None] - sin_o[:, None, :] * sin_i[None]
    table = table.reshape(width, width)
    sign = np.where(first, 0.0, 1.0 - 2.0 * part).astype(np.float32)
    weight = np.where(first, 1.0, 2.0).astype(np.float32)
    return halves(table), freq, sign, weight


def dot3(left, right_halves, contract):
    high, low = halves(left)
    right_high, right_low = right_halves
    count = left.shape[0]

    def dot(a, b):
        return lax.dot_general(
            a, b, (((1,), (contract,)), ((), ())), preferred_element_type=jnp.float32
        )

    both = dot(jnp.concatenate([high, low], axis=0), right_high)
    return both[:count] + both[count:] + dot(high, right_low)


def on_device(za, zb, w_in, b_in, w_out, b_out, unmix, kern):
    slab, quarter, width = za.shape
    hidden_local = w_in.shape[3]
    chans = unmix.shape[0]
    half = chans // 2
    rows = lax.axis_size("rows")
    groups = lax.axis_size("chan")
    row_idx = lax.axis_index("rows")
    chan_idx = lax.axis_index("chan")
    height = slab * rows
    block = width // groups
    mine = chans // groups
    lanes = 64
    freq_groups = width // lanes
    chan_groups = rows // freq_groups
    triple = mine // chan_groups

    table, freq, sign, weight = column_tables(width, lanes // 2)

    zb_cols = zb.reshape(slab, quarter, groups, block).transpose(2, 0, 1, 3)
    za_got, zb_got = gather(za, zb_cols, rows, groups)
    za_ext = za_got.transpose(0, 2, 1, 3, 4).reshape(3 * slab, half, width)
    ext_rows = row_idx * slab - slab + jnp.arange(3 * slab, dtype=jnp.int32)
    inside = (ext_rows >= 0) & (ext_rows < height)
    za_ext = jnp.where(inside[:, None, None], za_ext, jnp.zeros((), za.dtype))
    hidden = jax.nn.relu(conv_rows(za_ext, w_in) + b_in[None, :, None])
    hidden = jnp.where(inside[1:-1][:, None, None], hidden, 0.0).astype(jnp.bfloat16)
    w_flat = w_out.reshape(3, 3, hidden_local, chans)
    share = conv_rows(hidden, w_flat).astype(jnp.bfloat16)
    share = share.reshape(slab, chans, groups, block).transpose(2, 0, 1, 3)
    raw = jnp.sum(swap(share, "chan", 1).astype(jnp.float32), axis=0)
    raw = raw + b_out.reshape(chans)[None, :, None]
    latent = zb_got.transpose(1, 0, 2, 3).reshape(slab, half, block).astype(jnp.float32)
    coupled = (latent - raw[:, half:]) * jnp.exp(-jnp.tanh(raw[:, :half]))
    za_cols = lax.dynamic_slice_in_dim(za_ext[slab : 2 * slab], chan_idx * block, block, 2)
    joined = jnp.concatenate([za_cols.astype(jnp.float32), coupled], axis=1)
    mixed = jnp.einsum("oc,rcw->row", unmix, joined, precision=lax.Precision.HIGHEST)
    mixed = mixed.reshape(slab, groups, mine, block).transpose(1, 0, 2, 3)
    mixed = swap(mixed, "chan", 2)
    mixed = mixed.transpose(1, 2, 0, 3).reshape(slab * mine, width)

    packed = dot3(mixed, table, 0)
    outgoing = packed.reshape(slab, chan_groups, triple, freq_groups, lanes)
    outgoing = outgoing.transpose(3, 1, 2, 0, 4).reshape(rows, triple, slab * lanes)
    got = swap(outgoing, "rows", 3)
    data = got.reshape(rows, triple, slab, lanes).transpose(2, 0, 1, 3)
    data = data.reshape(height, triple, lanes)

    freq_idx = row_idx // chan_groups
    chan_first = chan_idx * mine + row_idx % chan_groups * triple

    def own_lanes(values):
        return lax.dynamic_slice_in_dim(jnp.asarray(values), freq_idx * lanes, lanes, 0)

    sign_own = own_lanes(sign)
    other = jnp.concatenate([data[..., lanes // 2 :], data[..., : lanes // 2]], axis=2)
    pair = jnp.concatenate([data, other * sign_own], axis=2).reshape(height, triple * 2 * lanes)
    order = (np.arange(rows)[None, :] * slab + np.arange(slab)[:, None]).reshape(-1)
    angles = np.arange(height)[:, None] * order[None, :] % height * (full_turn / height)
    cosine = np.cos(angles).astype(np.float32)
    sine = np.sin(angles).astype(np.float32)
    both = jnp.dot(
        jnp.asarray(np.concatenate([cosine, sine], axis=0)), pair, precision=lax.Precision.HIGH
    ).reshape(2, height, triple, 2, lanes)
    real_part = both[0, :, :, 0] + both[1, :, :, 1]
    imag_part = both[0, :, :, 1] - both[1, :, :, 0]

    turn = freq * (full_turn / width)
    cos_v = own_lanes(np.cos(turn).astype(np.float32))[None, None, :]
    sin_v = own_lanes(np.sin(turn).astype(np.float32))[None, None, :]
    stencil = lax.dynamic_slice_in_dim(kern, chan_first, triple, 2)[..., None]
    near_real = stencil[:, 1] + (stencil[:, 0] + stencil[:, 2]) * cos_v
    near_imag = (stencil[:, 2] - stencil[:, 0]) * sin_v
    row_turn = np.arange(height) * (full_turn / height)
    cos_u = jnp.asarray(np.cos(row_turn).astype(np.float32))[:, None, None]
    sin_u = jnp.asarray(np.sin(row_turn).astype(np.float32))[:, None, None]
    symbol_real = (
        near_real[1] + (near_real[0] + near_real[2]) * cos_u + (near_imag[0] - near_imag[2]) * sin_u
    )
    symbol_imag = (
        near_imag[1] + (near_imag[0] + near_imag[2]) * cos_u + (near_real[2] - near_real[0]) * sin_u
    )
    scale = own_lanes(weight) * (1.0 / (height * width))
    factor = scale / (symbol_real * symbol_real + symbol_imag * symbol_imag)
    solved_real = (real_part * symbol_real + imag_part * symbol_imag) * factor
    solved_imag = (imag_part * symbol_real - real_part * symbol_imag) * factor
    solved = jnp.concatenate([solved_real, solved_imag], axis=0).reshape(2 * height, triple * lanes)
    back_table = np.concatenate([cosine.T, -sine.T], axis=1)
    rows_back = jnp.dot(jnp.asarray(back_table), solved, precision=lax.Precision.HIGH)
    rows_back = rows_back.reshape(slab, rows, triple, lanes).transpose(1, 2, 0, 3)
    rows_back = swap(rows_back.reshape(rows, triple, slab * lanes), "rows", 4)
    final = rows_back.reshape(freq_groups, chan_groups, triple, slab, lanes)
    final = final.transpose(3, 1, 2, 0, 4).reshape(slab * mine, width)
    return dot3(final, table, 1).reshape(slab, mine, width)


def solution(mesh):
    placed = (
        P("rows", "chan", None),
        P("rows", "chan", None),
        P(None, None, None, "chan"),
        P("chan"),
        P(None, None, "chan", None, None),
        P(),
        P(),
        P(),
    )
    return jax.shard_map(
        on_device, mesh=mesh, in_specs=placed, out_specs=P("rows", "chan", None), check_vma=False
    )
```

```python
import math

import jax
import jax.numpy as jnp
import numpy as np
from jax import lax
from jax.experimental import pallas as pl
from jax.experimental.pallas import tpu as pltpu
from jax.sharding import PartitionSpec as P

full_turn = 2.0 * math.pi
vmem = pl.BlockSpec(memory_space=pltpu.VMEM)
mesh_ids = pl.DeviceIdType.MESH


def swap_kernel(axis, count, x_ref, out_ref, send_sem, recv_sem, own_sem):
    me_row = lax.axis_index("rows")
    me_chan = lax.axis_index("chan")
    me = me_row if axis == "rows" else me_chan

    def place(peer):
        return (peer, me_chan) if axis == "rows" else (me_row, peer)

    barrier = pltpu.get_barrier_semaphore()

    def greet(step, carry):
        pl.semaphore_signal(
            barrier, inc=1, device_id=place(lax.rem(me + step, count)), device_id_type=mesh_ids
        )
        return carry

    lax.fori_loop(1, count, greet, 0)
    own = pltpu.make_async_copy(x_ref.at[me], out_ref.at[me], own_sem)
    own.start()
    pl.semaphore_wait(barrier, count - 1)

    def copy(step):
        peer = lax.rem(me + step, count)
        return pltpu.make_async_remote_copy(
            src_ref=x_ref.at[peer],
            dst_ref=out_ref.at[me],
            send_sem=send_sem.at[step],
            recv_sem=recv_sem.at[step],
            device_id=place(peer),
            device_id_type=mesh_ids,
        )

    def start(step, carry):
        copy(step).start()
        return carry

    def finish(step, carry):
        copy(step).wait()
        return carry

    lax.fori_loop(1, count, start, 0)
    own.wait()
    lax.fori_loop(1, count, finish, 0)


def swap(x, axis, ident):
    count = x.shape[0]

    def kernel(*refs):
        swap_kernel(axis, count, *refs)

    return pl.pallas_call(
        kernel,
        out_shape=jax.ShapeDtypeStruct(x.shape, x.dtype),
        in_specs=[vmem],
        out_specs=vmem,
        scratch_shapes=[
            pltpu.SemaphoreType.DMA((count,)),
            pltpu.SemaphoreType.DMA((count,)),
            pltpu.SemaphoreType.DMA,
        ],
        compiler_params=pltpu.CompilerParams(collective_id=ident, has_side_effects=True),
        name="swap_" + axis + str(ident),
    )(x)


def gather_kernel(rows, chans, halves_of, *refs):
    za_ref, zb_ref, win_ref, wout_ref, bias_ref = refs[:5]
    za_out, zb_out, win_out, wout_out, bias_out = refs[5:10]
    za_sems, zb_sems, w_sems, pass_sems, own_sem = refs[10:]
    me_row = lax.axis_index("rows")
    me_chan = lax.axis_index("chan")
    core = lax.rem(me_row, 2)
    side = lax.rem(me_row // 2, halves_of)
    ring = halves_of * chans
    spot = side * chans + me_chan
    partner = (me_row + 1 - 2 * core, me_chan)
    barrier = pltpu.get_barrier_semaphore()
    peers = [(dr, dc) for dr in (0, 1, 2) for dc in range(chans) if (dr, dc) != (1, 0)]
    steps = (1, ring - 1, 2 + core * (ring - 4))

    def place(dr, dc):
        return (lax.rem(me_row + dr + rows - 1, rows), lax.rem(me_chan + dc, chans))

    def around(step):
        there = lax.rem(spot + step, ring)
        return (me_row + (there // chans - side) * 2, lax.rem(there, chans))

    for step in steps:
        pl.semaphore_signal(
            barrier, inc=1, device_id=around(ring - step), device_id_type=mesh_ids
        )
    for dr, dc in peers:
        pl.semaphore_signal(barrier, inc=1, device_id=place(dr, dc), device_id_type=mesh_ids)
    own = [
        pltpu.make_async_copy(win_ref, win_out.at[me_chan], own_sem.at[0]),
        pltpu.make_async_copy(wout_ref, wout_out.at[me_chan], own_sem.at[1]),
        pltpu.make_async_copy(za_ref.at[me_chan], za_out.at[1, me_chan], own_sem.at[2]),
        pltpu.make_async_copy(zb_ref.at[me_chan], zb_out.at[me_chan], own_sem.at[3]),
        pltpu.make_async_copy(bias_ref, bias_out.at[me_chan], own_sem.at[4]),
    ]
    for one in own:
        one.start()
    pl.semaphore_wait(barrier, len(peers) + len(steps))
    first = []
    for idx, step in enumerate(steps):
        for kind, (source, target) in enumerate(((wout_ref, wout_out), (win_ref, win_out))):
            first.append(
                pltpu.make_async_remote_copy(
                    src_ref=source.at[core],
                    dst_ref=target.at[me_chan, core],
                    send_sem=w_sems.at[0, kind, idx],
                    recv_sem=w_sems.at[1, kind, idx],
                    device_id=around(step),
                    device_id_type=mesh_ids,
                )
            )
    copies = []
    for idx, (dr, dc) in enumerate(peers):
        there = place(dr, dc)
        copies.append(
            pltpu.make_async_remote_copy(
                src_ref=za_ref.at[there[1]],
                dst_ref=za_out.at[2 - dr, me_chan],
                send_sem=za_sems.at[0, idx],
                recv_sem=za_sems.at[1, idx],
                device_id=there,
                device_id_type=mesh_ids,
            )
        )
    for dc in range(1, chans):
        peer = lax.rem(me_chan + dc, chans)
        pairs = ((zb_ref.at[peer], zb_out), (bias_ref, bias_out))
        for kind, (source, target) in enumerate(pairs):
            copies.append(
                pltpu.make_async_remote_copy(
                    src_ref=source,
                    dst_ref=target.at[me_chan],
                    send_sem=zb_sems.at[0, kind, dc],
                    recv_sem=zb_sems.at[1, kind, dc],
                    device_id=(me_row, peer),
                    device_id_type=mesh_ids,
                )
            )
    for one in first:
        one.start()
    for one in copies:
        one.start()
    passed = []
    for idx, step in enumerate(steps):
        origin = lax.rem(spot + ring - step, ring)
        quarter = lax.rem(origin, chans)
        for kind, target in enumerate((wout_out, win_out)):
            first[2 * idx + kind].wait_recv()
            one = pltpu.make_async_remote_copy(
                src_ref=target.at[quarter, core],
                dst_ref=target.at[quarter, core],
                send_sem=pass_sems.at[0, kind, idx],
                recv_sem=pass_sems.at[1, kind, idx],
                device_id=partner,
                device_id_type=mesh_ids,
            )
            one.start()
            passed.append(one)
    for one in own:
        one.wait()
    for one in copies:
        one.wait()
    for one in passed:
        one.wait()
    for one in first:
        one.wait_send()


def gather(za_cols, zb_cols, w_in, w_out, bias, rows, chans, halves_of):
    def kernel(*refs):
        gather_kernel(rows, chans, halves_of, *refs)

    def several(lead, x):
        return jax.ShapeDtypeStruct(lead + x.shape, x.dtype)

    return pl.pallas_call(
        kernel,
        out_shape=(
            several((3,), za_cols),
            several((), zb_cols),
            several((chans,), w_in),
            several((chans,), w_out),
            several((chans,), bias),
        ),
        in_specs=[vmem] * 5,
        out_specs=(vmem,) * 5,
        scratch_shapes=[
            pltpu.SemaphoreType.DMA((2, 3 * chans)),
            pltpu.SemaphoreType.DMA((2, 2, chans)),
            pltpu.SemaphoreType.DMA((2, 2, 3)),
            pltpu.SemaphoreType.DMA((2, 2, 3)),
            pltpu.SemaphoreType.DMA((5,)),
        ],
        compiler_params=pltpu.CompilerParams(collective_id=0, has_side_effects=True),
        name="gather_inputs",
    )(za_cols, zb_cols, w_in, w_out, bias)


def taps_of(source, width):
    rows_out = source.shape[0] - 2
    pieces = [
        source[row_off : row_off + rows_out, :, col_off : col_off + width]
        for row_off in range(3)
        for col_off in range(3)
    ]
    return jnp.stack(pieces, axis=1)


def halves(values):
    high = lax.reduce_precision(values, 8, 7)
    return high.astype(jnp.bfloat16), (values - high).astype(jnp.bfloat16)


def column_tables(width, group):
    pos = np.arange(width)
    part = pos // group % 2
    slot = pos // (2 * group) * group + pos % group
    first = slot == 0
    freq = np.where(first & (part == 1), width // 2, slot)
    shift = np.where(first, 0, part) * (math.pi / 2)
    fine = 32
    outer = (np.arange(width // fine) * fine)[:, None] * freq[None, :] % width * (full_turn / width)
    inner = np.arange(fine)[:, None] * freq[None, :] % width * (full_turn / width) + shift[None, :]
    consts = [f(a).astype(np.float32) for a in (outer, inner) for f in (np.cos, np.sin)]
    cos_o, sin_o, cos_i, sin_i = lax.optimization_barrier(tuple(jnp.asarray(c) for c in consts))
    table = cos_o[:, None, :] * cos_i[None] - sin_o[:, None, :] * sin_i[None]
    table = table.reshape(width, width)
    sign = np.where(first, 0.0, 1.0 - 2.0 * part).astype(np.float32)
    weight = np.where(first, 1.0, 2.0).astype(np.float32)
    return halves(table), freq, sign, weight


def dot3(left, right_halves, contract):
    high, low = halves(left)
    right_high, right_low = right_halves
    count = left.shape[0]

    def dot(a, b):
        return lax.dot_general(
            a, b, (((1,), (contract,)), ((), ())), preferred_element_type=jnp.float32
        )

    both = dot(jnp.concatenate([high, low], axis=0), right_high)
    return both[:count] + both[count:] + dot(high, right_low)


def on_device(za, zb, w_in, b_in, w_out, b_out, unmix, kern):
    slab, quarter, width = za.shape
    hidden_local = w_in.shape[3]
    chans = unmix.shape[0]
    half = chans // 2
    rows = lax.axis_size("rows")
    groups = lax.axis_size("chan")
    row_idx = lax.axis_index("rows")
    chan_idx = lax.axis_index("chan")
    height = slab * rows
    block = width // groups
    mine = chans // groups
    lanes = 64
    freq_groups = width // lanes
    chan_groups = rows // freq_groups
    triple = mine // chan_groups

    table, freq, sign, weight = column_tables(width, lanes // 2)

    zb_cols = zb.reshape(slab * quarter, groups, block).transpose(1, 0, 2)
    za_wide = jnp.pad(za.reshape(slab * quarter, width), ((0, 0), (2, 128 + 2)))
    za_cols = jnp.stack(
        [za_wide[:, block * i : block * i + block + 128] for i in range(groups)], axis=0
    )
    taps = 9
    w_in_parts = w_in.reshape(2, taps * half // 2, hidden_local)
    w_out_parts = w_out.reshape(taps * hidden_local, chans).T.reshape(
        2, chans // 2, taps * hidden_local
    )
    za_got, zb_got, w_in_all, w_out_all, bias = gather(
        za_cols, zb_cols, w_in_parts, w_out_parts, b_in[None, :], rows, groups, 2
    )
    za_ext = za_got.reshape(3, groups, slab, quarter, block + 128)[..., : block + 4]
    za_ext = za_ext.transpose(0, 2, 1, 3, 4).reshape(3 * slab, half, block + 4)
    ext_rows = row_idx * slab - slab + jnp.arange(3 * slab, dtype=jnp.int32)
    inside = (ext_rows >= 0) & (ext_rows < height)
    za_ext = jnp.where(inside[:, None, None], za_ext, jnp.zeros((), za.dtype))
    ext_cols = chan_idx * block - 1 + jnp.arange(block + 2, dtype=jnp.int32)
    inside_cols = (ext_cols >= 0) & (ext_cols < width)
    hidden_units = groups * hidden_local
    hidden = jnp.einsum(
        "rkcw,qkco->rqow",
        taps_of(za_ext, block + 2),
        w_in_all.reshape(groups, taps, half, hidden_local),
        preferred_element_type=jnp.float32,
    ).reshape(2 * slab, hidden_units, block + 2)
    hidden = jax.nn.relu(hidden + bias.reshape(hidden_units)[None, :, None])
    keep = inside[1:-1][:, None, None] & inside_cols[None, None, :]
    hidden = jnp.where(keep, hidden, 0.0).astype(jnp.bfloat16)
    hidden_taps = taps_of(hidden, block).reshape(slab, taps, groups, hidden_local, block)
    raw = jnp.einsum(
        "rkqcw,qokc->row",
        hidden_taps,
        w_out_all.reshape(groups, chans, taps, hidden_local),
        preferred_element_type=jnp.float32,
    )
    raw = raw + b_out.reshape(chans)[None, :, None]
    latent = zb_got.reshape(groups, slab, quarter, block).transpose(1, 0, 2, 3)
    latent = latent.reshape(slab, half, block).astype(jnp.float32)
    coupled = (latent - raw[:, half:]) * jnp.exp(-jnp.tanh(raw[:, :half]))
    za_own = za_ext[slab : 2 * slab, :, 2 : 2 + block]
    joined = jnp.concatenate([za_own.astype(jnp.float32), coupled], axis=1)
    mixed = jnp.einsum("oc,rcw->row", unmix, joined, precision=lax.Precision.HIGHEST)
    mixed = mixed.reshape(slab, groups, mine, block).transpose(1, 0, 2, 3)
    mixed = swap(mixed, "chan", 1)
    mixed = mixed.transpose(1, 2, 0, 3).reshape(slab * mine, width)

    packed = dot3(mixed, table, 0)
    outgoing = packed.reshape(slab, chan_groups, triple, freq_groups, lanes)
    outgoing = outgoing.transpose(3, 1, 2, 0, 4).reshape(rows, triple, slab * lanes)
    got = swap(outgoing, "rows", 3)
    data = got.reshape(rows, triple, slab, lanes).transpose(2, 0, 1, 3)
    data = data.reshape(height, triple, lanes)

    freq_idx = row_idx // chan_groups
    chan_first = chan_idx * mine + row_idx % chan_groups * triple

    def own_lanes(values):
        grouped = jnp.asarray(values).reshape(freq_groups, lanes)
        return lax.dynamic_index_in_dim(grouped, freq_idx, 0, keepdims=False)

    sign_own = own_lanes(sign)
    other = jnp.concatenate([data[..., lanes // 2 :], data[..., : lanes // 2]], axis=2)
    pair = jnp.concatenate([data, other * sign_own], axis=2).reshape(height, triple * 2 * lanes)
    order = (np.arange(rows)[None, :] * slab + np.arange(slab)[:, None]).reshape(-1)
    angles = np.arange(height)[:, None] * order[None, :] % height * (full_turn / height)
    cosine = np.cos(angles).astype(np.float32)
    sine = np.sin(angles).astype(np.float32)
    both = jnp.dot(
        jnp.asarray(np.concatenate([cosine, sine], axis=0)), pair, precision=lax.Precision.HIGH
    ).reshape(2, height, triple, 2, lanes)
    real_part = both[0, :, :, 0] + both[1, :, :, 1]
    imag_part = both[0, :, :, 1] - both[1, :, :, 0]

    turn = freq * (full_turn / width)
    cos_v = own_lanes(np.cos(turn).astype(np.float32))[None, None, :]
    sin_v = own_lanes(np.sin(turn).astype(np.float32))[None, None, :]
    stencil = lax.dynamic_slice_in_dim(kern, chan_first, triple, 2)[..., None]
    near_real = stencil[:, 1] + (stencil[:, 0] + stencil[:, 2]) * cos_v
    near_imag = (stencil[:, 2] - stencil[:, 0]) * sin_v
    row_turn = np.arange(height) * (full_turn / height)
    cos_u = jnp.asarray(np.cos(row_turn).astype(np.float32))[:, None, None]
    sin_u = jnp.asarray(np.sin(row_turn).astype(np.float32))[:, None, None]
    symbol_real = (
        near_real[1] + (near_real[0] + near_real[2]) * cos_u + (near_imag[0] - near_imag[2]) * sin_u
    )
    symbol_imag = (
        near_imag[1] + (near_imag[0] + near_imag[2]) * cos_u + (near_real[2] - near_real[0]) * sin_u
    )
    scale = own_lanes(weight) * (1.0 / (height * width))
    factor = scale / (symbol_real * symbol_real + symbol_imag * symbol_imag)
    solved_real = (real_part * symbol_real + imag_part * symbol_imag) * factor
    solved_imag = (imag_part * symbol_real - real_part * symbol_imag) * factor
    solved = jnp.concatenate([solved_real, solved_imag], axis=0).reshape(2 * height, triple * lanes)
    back_table = np.concatenate([cosine.T, -sine.T], axis=1)
    rows_back = jnp.dot(jnp.asarray(back_table), solved, precision=lax.Precision.HIGH)
    rows_back = rows_back.reshape(slab, rows, triple, lanes).transpose(1, 2, 0, 3)
    rows_back = swap(rows_back.reshape(rows, triple, slab * lanes), "rows", 4)
    final = rows_back.reshape(freq_groups, chan_groups, triple, slab, lanes)
    final = final.transpose(3, 1, 2, 0, 4).reshape(slab * mine, width)
    return dot3(final, table, 1).reshape(slab, mine, width)


def solution(mesh):
    placed = (
        P("rows", "chan", None),
        P("rows", "chan", None),
        P(None, None, None, "chan"),
        P("chan"),
        P(None, None, "chan", None, None),
        P(),
        P(),
        P(),
    )
    return jax.shard_map(
        on_device, mesh=mesh, in_specs=placed, out_specs=P("rows", "chan", None), check_vma=False
    )
```

```python
import math

import jax
import jax.numpy as jnp
import numpy as np
from jax import lax
from jax.experimental import pallas as pl
from jax.experimental.pallas import tpu as pltpu
from jax.sharding import PartitionSpec as P

full_turn = 2.0 * math.pi
vmem = pl.BlockSpec(memory_space=pltpu.VMEM)
mesh_ids = pl.DeviceIdType.MESH


def swap_kernel(axis, count, x_ref, out_ref, send_sem, recv_sem, own_sem):
    me_row = lax.axis_index("rows")
    me_chan = lax.axis_index("chan")
    me = me_row if axis == "rows" else me_chan

    def place(peer):
        return (peer, me_chan) if axis == "rows" else (me_row, peer)

    barrier = pltpu.get_barrier_semaphore()

    def greet(step, carry):
        pl.semaphore_signal(
            barrier, inc=1, device_id=place(lax.rem(me + step, count)), device_id_type=mesh_ids
        )
        return carry

    lax.fori_loop(1, count, greet, 0)
    own = pltpu.make_async_copy(x_ref.at[me], out_ref.at[me], own_sem)
    own.start()
    pl.semaphore_wait(barrier, count - 1)

    def copy(step):
        peer = lax.rem(me + step, count)
        return pltpu.make_async_remote_copy(
            src_ref=x_ref.at[peer],
            dst_ref=out_ref.at[me],
            send_sem=send_sem.at[step],
            recv_sem=recv_sem.at[step],
            device_id=place(peer),
            device_id_type=mesh_ids,
        )

    def start(step, carry):
        copy(step).start()
        return carry

    def finish(step, carry):
        copy(step).wait()
        return carry

    lax.fori_loop(1, count, start, 0)
    own.wait()
    lax.fori_loop(1, count, finish, 0)


def swap(x, axis, ident):
    count = x.shape[0]

    def kernel(*refs):
        swap_kernel(axis, count, *refs)

    return pl.pallas_call(
        kernel,
        out_shape=jax.ShapeDtypeStruct(x.shape, x.dtype),
        in_specs=[vmem],
        out_specs=vmem,
        scratch_shapes=[
            pltpu.SemaphoreType.DMA((count,)),
            pltpu.SemaphoreType.DMA((count,)),
            pltpu.SemaphoreType.DMA,
        ],
        compiler_params=pltpu.CompilerParams(collective_id=ident, has_side_effects=True),
        name="swap_" + axis + str(ident),
    )(x)


def gather_kernel(rows, chans, halves_of, *refs):
    za_ref, zb_ref, win_ref, wout_ref, bias_ref = refs[:5]
    za_out, zb_out, win_out, wout_out, bias_out = refs[5:10]
    za_sems, zb_sems, w_sems, pass_sems, own_sem = refs[10:]
    me_row = lax.axis_index("rows")
    me_chan = lax.axis_index("chan")
    core = lax.rem(me_row, 2)
    side = lax.rem(me_row // 2, halves_of)
    ring = halves_of * chans
    spot = side * chans + me_chan
    partner = (me_row + 1 - 2 * core, me_chan)
    barrier = pltpu.get_barrier_semaphore()
    peers = [(dr, dc) for dr in (0, 1, 2) for dc in range(chans) if (dr, dc) != (1, 0)]
    steps = (1, ring - 1, 2 + core * (ring - 4))

    def place(dr, dc):
        return (lax.rem(me_row + dr + rows - 1, rows), lax.rem(me_chan + dc, chans))

    def around(step):
        there = lax.rem(spot + step, ring)
        return (me_row + (there // chans - side) * 2, lax.rem(there, chans))

    for step in steps:
        pl.semaphore_signal(
            barrier, inc=1, device_id=around(ring - step), device_id_type=mesh_ids
        )
    for dr, dc in peers:
        pl.semaphore_signal(barrier, inc=1, device_id=place(dr, dc), device_id_type=mesh_ids)
    own = [
        pltpu.make_async_copy(win_ref, win_out.at[me_chan], own_sem.at[0]),
        pltpu.make_async_copy(wout_ref, wout_out.at[me_chan], own_sem.at[1]),
        pltpu.make_async_copy(za_ref.at[me_chan], za_out.at[1, me_chan], own_sem.at[2]),
        pltpu.make_async_copy(zb_ref.at[me_chan], zb_out.at[me_chan], own_sem.at[3]),
        pltpu.make_async_copy(bias_ref, bias_out.at[me_chan], own_sem.at[4]),
    ]
    for one in own:
        one.start()
    pl.semaphore_wait(barrier, len(peers) + len(steps))
    first = []
    for idx, step in enumerate(steps):
        for kind, (source, target) in enumerate(((wout_ref, wout_out), (win_ref, win_out))):
            first.append(
                pltpu.make_async_remote_copy(
                    src_ref=source.at[core],
                    dst_ref=target.at[me_chan, core],
                    send_sem=w_sems.at[0, kind, idx],
                    recv_sem=w_sems.at[1, kind, idx],
                    device_id=around(step),
                    device_id_type=mesh_ids,
                )
            )
    copies = []
    for idx, (dr, dc) in enumerate(peers):
        there = place(dr, dc)
        copies.append(
            pltpu.make_async_remote_copy(
                src_ref=za_ref.at[there[1]],
                dst_ref=za_out.at[2 - dr, me_chan],
                send_sem=za_sems.at[0, idx],
                recv_sem=za_sems.at[1, idx],
                device_id=there,
                device_id_type=mesh_ids,
            )
        )
    for dc in range(1, chans):
        peer = lax.rem(me_chan + dc, chans)
        pairs = ((zb_ref.at[peer], zb_out), (bias_ref, bias_out))
        for kind, (source, target) in enumerate(pairs):
            copies.append(
                pltpu.make_async_remote_copy(
                    src_ref=source,
                    dst_ref=target.at[me_chan],
                    send_sem=zb_sems.at[0, kind, dc],
                    recv_sem=zb_sems.at[1, kind, dc],
                    device_id=(me_row, peer),
                    device_id_type=mesh_ids,
                )
            )
    for one in first:
        one.start()
    for one in copies:
        one.start()
    passed = []
    for idx, step in enumerate(steps):
        origin = lax.rem(spot + ring - step, ring)
        quarter = lax.rem(origin, chans)
        for kind, target in enumerate((wout_out, win_out)):
            first[2 * idx + kind].wait_recv()
            one = pltpu.make_async_remote_copy(
                src_ref=target.at[quarter, core],
                dst_ref=target.at[quarter, core],
                send_sem=pass_sems.at[0, kind, idx],
                recv_sem=pass_sems.at[1, kind, idx],
                device_id=partner,
                device_id_type=mesh_ids,
            )
            one.start()
            passed.append(one)
    for one in own:
        one.wait()
    for one in copies:
        one.wait()
    for one in passed:
        one.wait()
    for one in first:
        one.wait_send()


def gather(za_cols, zb_cols, w_in, w_out, bias, rows, chans, halves_of):
    def kernel(*refs):
        gather_kernel(rows, chans, halves_of, *refs)

    def several(lead, x):
        return jax.ShapeDtypeStruct(lead + x.shape, x.dtype)

    return pl.pallas_call(
        kernel,
        out_shape=(
            several((3,), za_cols),
            several((), zb_cols),
            several((chans,), w_in),
            several((chans,), w_out),
            several((chans,), bias),
        ),
        in_specs=[vmem] * 5,
        out_specs=(vmem,) * 5,
        scratch_shapes=[
            pltpu.SemaphoreType.DMA((2, 3 * chans)),
            pltpu.SemaphoreType.DMA((2, 2, chans)),
            pltpu.SemaphoreType.DMA((2, 2, 3)),
            pltpu.SemaphoreType.DMA((2, 2, 3)),
            pltpu.SemaphoreType.DMA((5,)),
        ],
        compiler_params=pltpu.CompilerParams(collective_id=0, has_side_effects=True),
        name="gather_inputs",
    )(za_cols, zb_cols, w_in, w_out, bias)


def couple_kernel(dims, *refs):
    slab, half, quarter, hidden_local, groups, block, width, height = dims
    za_ref, zb_ref, win_ref, wout_ref, bias_ref, bout_ref, unmix_ref, out_ref = refs[:8]
    taps_ref, hidden_ref = refs[8:]
    wide = za_ref.shape[2]
    first_row = lax.axis_index("rows") * slab - slab
    first_col = lax.axis_index("chan") * block - 1
    span = 3 * half
    for row in range(3 * slab):
        plane = za_ref[row].astype(jnp.float32)
        for off in range(3):
            moved = plane if off == 0 else pltpu.roll(plane, wide - off, 1)
            taps_ref[pl.ds(row * span + off * half, half), :] = moved.astype(jnp.bfloat16)
    cols = first_col + lax.broadcasted_iota(jnp.int32, (hidden_local, wide), 1)
    inside = (cols >= 0) & (cols < width)
    deep = 3 * hidden_local
    for row in range(2 * slab):
        line = first_row + row + 1
        keep = inside & (line >= 0) & (line < height)
        stack = taps_ref[pl.ds(row * span, 3 * span), :]
        for part in range(groups):
            value = lax.dot_general(
                win_ref[part], stack, (((0,), (0,)), ((), ())), preferred_element_type=jnp.float32
            )
            value = jnp.maximum(value + bias_ref[pl.ds(part * hidden_local, hidden_local), :], 0.0)
            value = jnp.where(keep, value, 0.0)
            for off in range(3):
                moved = value if off == 0 else pltpu.roll(value, wide - off, 1)
                hidden_ref[part, pl.ds(row * deep + off * hidden_local, hidden_local), :] = moved[
                    :, :block
                ].astype(jnp.bfloat16)
    share = unmix_ref.shape[0] // groups
    for row in range(slab):
        raw = bout_ref[...] + jnp.zeros((2 * half, block), jnp.float32)
        for part in range(groups):
            raw = raw + jnp.dot(
                wout_ref[part],
                hidden_ref[part, pl.ds(row * deep, 3 * deep), :],
                preferred_element_type=jnp.float32,
            )
        latent = zb_ref[row].astype(jnp.float32)
        coupled = (latent - raw[half:]) * jnp.exp(-jnp.tanh(raw[:half]))
        own = pltpu.roll(za_ref[slab + row].astype(jnp.float32), wide - 2, 1)[:, :block]
        joined = jnp.concatenate([own, coupled], axis=0)
        mixed = jnp.dot(
            unmix_ref[...],
            joined,
            precision=lax.Precision.HIGHEST,
            preferred_element_type=jnp.float32,
        )
        for part in range(groups):
            out_ref[part, pl.ds(row * share, share), :] = mixed[part * share : (part + 1) * share]


def couple(za_ext, latent, w_in, w_out, bias, b_out, unmix, dims):
    slab, half, quarter, hidden_local, groups, block, width, height = dims
    wide = za_ext.shape[2]
    chans = unmix.shape[0]

    def kernel(*refs):
        couple_kernel(dims, *refs)

    return pl.pallas_call(
        kernel,
        out_shape=jax.ShapeDtypeStruct((groups, slab * chans // groups, block), jnp.float32),
        in_specs=[vmem] * 7,
        out_specs=vmem,
        scratch_shapes=[
            pltpu.VMEM((3 * slab * 3 * half, wide), jnp.bfloat16),
            pltpu.VMEM((groups, 2 * slab * 3 * hidden_local, block), jnp.bfloat16),
        ],
        name="couple_and_mix",
    )(za_ext, latent, w_in, w_out, bias, b_out, unmix)


def halves(values):
    high = lax.reduce_precision(values, 8, 7)
    return high.astype(jnp.bfloat16), (values - high).astype(jnp.bfloat16)


def column_tables(width, group):
    pos = np.arange(width)
    part = pos // group % 2
    slot = pos // (2 * group) * group + pos % group
    first = slot == 0
    freq = np.where(first & (part == 1), width // 2, slot)
    shift = np.where(first, 0, part) * (math.pi / 2)
    fine = 32
    outer = (np.arange(width // fine) * fine)[:, None] * freq[None, :] % width * (full_turn / width)
    inner = np.arange(fine)[:, None] * freq[None, :] % width * (full_turn / width) + shift[None, :]
    consts = [f(a).astype(np.float32) for a in (outer, inner) for f in (np.cos, np.sin)]
    cos_o, sin_o, cos_i, sin_i = lax.optimization_barrier(tuple(jnp.asarray(c) for c in consts))
    table = cos_o[:, None, :] * cos_i[None] - sin_o[:, None, :] * sin_i[None]
    table = table.reshape(width, width)
    sign = np.where(first, 0.0, 1.0 - 2.0 * part).astype(np.float32)
    weight = np.where(first, 1.0, 2.0).astype(np.float32)
    return halves(table), freq, sign, weight


def dot3(left, right_halves, contract):
    high, low = halves(left)
    right_high, right_low = right_halves
    count = left.shape[0]

    def dot(a, b):
        return lax.dot_general(
            a, b, (((1,), (contract,)), ((), ())), preferred_element_type=jnp.float32
        )

    both = dot(jnp.concatenate([high, low], axis=0), right_high)
    return both[:count] + both[count:] + dot(high, right_low)


def on_device(za, zb, w_in, b_in, w_out, b_out, unmix, kern):
    slab, quarter, width = za.shape
    hidden_local = w_in.shape[3]
    chans = unmix.shape[0]
    half = chans // 2
    rows = lax.axis_size("rows")
    groups = lax.axis_size("chan")
    row_idx = lax.axis_index("rows")
    chan_idx = lax.axis_index("chan")
    height = slab * rows
    block = width // groups
    mine = chans // groups
    lanes = 64
    freq_groups = width // lanes
    chan_groups = rows // freq_groups
    triple = mine // chan_groups

    table, freq, sign, weight = column_tables(width, lanes // 2)

    zb_cols = zb.reshape(slab * quarter, groups, block).transpose(1, 0, 2)
    za_wide = jnp.pad(za.reshape(slab * quarter, width), ((0, 0), (2, 128 + 2)))
    za_cols = jnp.stack(
        [za_wide[:, block * i : block * i + block + 128] for i in range(groups)], axis=0
    )
    taps = 9
    w_in_parts = w_in.reshape(2, taps * half // 2, hidden_local)
    w_out_parts = w_out.reshape(taps * hidden_local, chans).T.reshape(
        2, chans // 2, taps * hidden_local
    )
    za_got, zb_got, w_in_all, w_out_all, bias = gather(
        za_cols, zb_cols, w_in_parts, w_out_parts, b_in[None, :], rows, groups, 2
    )
    za_ext = za_got.reshape(3, groups, slab, quarter, block + 128)
    za_ext = za_ext.transpose(0, 2, 1, 3, 4).reshape(3 * slab, half, block + 128)
    ext_rows = row_idx * slab - slab + jnp.arange(3 * slab, dtype=jnp.int32)
    inside = (ext_rows >= 0) & (ext_rows < height)
    za_ext = jnp.where(inside[:, None, None], za_ext, jnp.zeros((), za.dtype))
    latent = zb_got.reshape(groups, slab, quarter, block).transpose(1, 0, 2, 3)
    mixed = couple(
        za_ext,
        latent.reshape(slab, half, block),
        w_in_all.reshape(groups, taps * half, hidden_local),
        w_out_all.reshape(groups, chans, taps * hidden_local),
        bias.reshape(groups * hidden_local, 1),
        b_out.reshape(chans, 1),
        unmix,
        (slab, half, quarter, hidden_local, groups, block, width, height),
    )
    mixed = swap(mixed, "chan", 1)
    mixed = mixed.transpose(1, 0, 2).reshape(slab * mine, width)

    packed = dot3(mixed, table, 0)
    outgoing = packed.reshape(slab, chan_groups, triple, freq_groups, lanes)
    outgoing = outgoing.transpose(3, 1, 2, 0, 4).reshape(rows, triple, slab * lanes)
    got = swap(outgoing, "rows", 3)
    data = got.reshape(rows, triple, slab, lanes).transpose(2, 0, 1, 3)
    data = data.reshape(height, triple, lanes)

    freq_idx = row_idx // chan_groups
    chan_first = chan_idx * mine + row_idx % chan_groups * triple

    def own_lanes(values):
        grouped = jnp.asarray(values).reshape(freq_groups, lanes)
        return lax.dynamic_index_in_dim(grouped, freq_idx, 0, keepdims=False)

    sign_own = own_lanes(sign)
    other = jnp.concatenate([data[..., lanes // 2 :], data[..., : lanes // 2]], axis=2)
    pair = jnp.concatenate([data, other * sign_own], axis=2).reshape(height, triple * 2 * lanes)
    order = (np.arange(rows)[None, :] * slab + np.arange(slab)[:, None]).reshape(-1)
    angles = np.arange(height)[:, None] * order[None, :] % height * (full_turn / height)
    cosine = np.cos(angles).astype(np.float32)
    sine = np.sin(angles).astype(np.float32)
    both = jnp.dot(
        jnp.asarray(np.concatenate([cosine, sine], axis=0)), pair, precision=lax.Precision.HIGH
    ).reshape(2, height, triple, 2, lanes)
    real_part = both[0, :, :, 0] + both[1, :, :, 1]
    imag_part = both[0, :, :, 1] - both[1, :, :, 0]

    turn = freq * (full_turn / width)
    cos_v = own_lanes(np.cos(turn).astype(np.float32))[None, None, :]
    sin_v = own_lanes(np.sin(turn).astype(np.float32))[None, None, :]
    stencil = lax.dynamic_slice_in_dim(kern, chan_first, triple, 2)[..., None]
    near_real = stencil[:, 1] + (stencil[:, 0] + stencil[:, 2]) * cos_v
    near_imag = (stencil[:, 2] - stencil[:, 0]) * sin_v
    row_turn = np.arange(height) * (full_turn / height)
    cos_u = jnp.asarray(np.cos(row_turn).astype(np.float32))[:, None, None]
    sin_u = jnp.asarray(np.sin(row_turn).astype(np.float32))[:, None, None]
    symbol_real = (
        near_real[1] + (near_real[0] + near_real[2]) * cos_u + (near_imag[0] - near_imag[2]) * sin_u
    )
    symbol_imag = (
        near_imag[1] + (near_imag[0] + near_imag[2]) * cos_u + (near_real[2] - near_real[0]) * sin_u
    )
    scale = own_lanes(weight) * (1.0 / (height * width))
    factor = scale / (symbol_real * symbol_real + symbol_imag * symbol_imag)
    solved_real = (real_part * symbol_real + imag_part * symbol_imag) * factor
    solved_imag = (imag_part * symbol_real - real_part * symbol_imag) * factor
    solved = jnp.concatenate([solved_real, solved_imag], axis=0).reshape(2 * height, triple * lanes)
    back_table = np.concatenate([cosine.T, -sine.T], axis=1)
    rows_back = jnp.dot(jnp.asarray(back_table), solved, precision=lax.Precision.HIGH)
    rows_back = rows_back.reshape(slab, rows, triple, lanes).transpose(1, 2, 0, 3)
    rows_back = swap(rows_back.reshape(rows, triple, slab * lanes), "rows", 4)
    final = rows_back.reshape(freq_groups, chan_groups, triple, slab, lanes)
    final = final.transpose(3, 1, 2, 0, 4).reshape(slab * mine, width)
    return dot3(final, table, 1).reshape(slab, mine, width)


def solution(mesh):
    placed = (
        P("rows", "chan", None),
        P("rows", "chan", None),
        P(None, None, None, "chan"),
        P("chan"),
        P(None, None, "chan", None, None),
        P(),
        P(),
        P(),
    )
    return jax.shard_map(
        on_device, mesh=mesh, in_specs=placed, out_specs=P("rows", "chan", None), check_vma=False
    )
```

```python
import math

import jax
import jax.numpy as jnp
import numpy as np
from jax import lax
from jax.experimental import pallas as pl
from jax.experimental.pallas import tpu as pltpu
from jax.sharding import PartitionSpec as P

full_turn = 2.0 * math.pi
vmem = pl.BlockSpec(memory_space=pltpu.VMEM)
mesh_ids = pl.DeviceIdType.MESH


def gather_kernel(rows, chans, halves_of, *refs):
    za_ref, zb_ref, win_ref, wout_ref, bias_ref = refs[:5]
    za_out, zb_out, win_out, wout_out, bias_out = refs[5:10]
    za_sems, zb_sems, w_sems, pass_sems, own_sem = refs[10:]
    me_row = lax.axis_index("rows")
    me_chan = lax.axis_index("chan")
    core = lax.rem(me_row, 2)
    side = lax.rem(me_row // 2, halves_of)
    ring = halves_of * chans
    spot = side * chans + me_chan
    partner = (me_row + 1 - 2 * core, me_chan)
    barrier = pltpu.get_barrier_semaphore()
    peers = [(dr, dc) for dr in (0, 1, 2) for dc in range(chans) if (dr, dc) != (1, 0)]
    steps = (1, ring - 1, 2 + core * (ring - 4))

    def place(dr, dc):
        return (lax.rem(me_row + dr + rows - 1, rows), lax.rem(me_chan + dc, chans))

    def around(step):
        there = lax.rem(spot + step, ring)
        return (me_row + (there // chans - side) * 2, lax.rem(there, chans))

    for step in steps:
        pl.semaphore_signal(
            barrier, inc=1, device_id=around(ring - step), device_id_type=mesh_ids
        )
    for dr, dc in peers:
        pl.semaphore_signal(barrier, inc=1, device_id=place(dr, dc), device_id_type=mesh_ids)
    own = [
        pltpu.make_async_copy(win_ref, win_out.at[me_chan], own_sem.at[0]),
        pltpu.make_async_copy(wout_ref, wout_out.at[me_chan], own_sem.at[1]),
        pltpu.make_async_copy(za_ref.at[me_chan], za_out.at[1, me_chan], own_sem.at[2]),
        pltpu.make_async_copy(zb_ref.at[me_chan], zb_out.at[me_chan], own_sem.at[3]),
        pltpu.make_async_copy(bias_ref, bias_out.at[me_chan], own_sem.at[4]),
    ]
    for one in own:
        one.start()
    pl.semaphore_wait(barrier, len(peers) + len(steps))
    first = []
    for idx, step in enumerate(steps):
        for kind, (source, target) in enumerate(((wout_ref, wout_out), (win_ref, win_out))):
            first.append(
                pltpu.make_async_remote_copy(
                    src_ref=source.at[core],
                    dst_ref=target.at[me_chan, core],
                    send_sem=w_sems.at[0, kind, idx],
                    recv_sem=w_sems.at[1, kind, idx],
                    device_id=around(step),
                    device_id_type=mesh_ids,
                )
            )
    copies = []
    for idx, (dr, dc) in enumerate(peers):
        there = place(dr, dc)
        copies.append(
            pltpu.make_async_remote_copy(
                src_ref=za_ref.at[there[1]],
                dst_ref=za_out.at[2 - dr, me_chan],
                send_sem=za_sems.at[0, idx],
                recv_sem=za_sems.at[1, idx],
                device_id=there,
                device_id_type=mesh_ids,
            )
        )
    for dc in range(1, chans):
        peer = lax.rem(me_chan + dc, chans)
        pairs = ((zb_ref.at[peer], zb_out), (bias_ref, bias_out))
        for kind, (source, target) in enumerate(pairs):
            copies.append(
                pltpu.make_async_remote_copy(
                    src_ref=source,
                    dst_ref=target.at[me_chan],
                    send_sem=zb_sems.at[0, kind, dc],
                    recv_sem=zb_sems.at[1, kind, dc],
                    device_id=(me_row, peer),
                    device_id_type=mesh_ids,
                )
            )
    for one in first:
        one.start()
    for one in copies:
        one.start()
    passed = []
    for idx, step in enumerate(steps):
        origin = lax.rem(spot + ring - step, ring)
        quarter = lax.rem(origin, chans)
        for kind, target in enumerate((wout_out, win_out)):
            first[2 * idx + kind].wait_recv()
            one = pltpu.make_async_remote_copy(
                src_ref=target.at[quarter, core],
                dst_ref=target.at[quarter, core],
                send_sem=pass_sems.at[0, kind, idx],
                recv_sem=pass_sems.at[1, kind, idx],
                device_id=partner,
                device_id_type=mesh_ids,
            )
            one.start()
            passed.append(one)
    for one in own:
        one.wait()
    for one in copies:
        one.wait()
    for one in passed:
        one.wait()
    for one in first:
        one.wait_send()


def gather(za_cols, zb_cols, w_in, w_out, bias, rows, chans, halves_of):
    def kernel(*refs):
        gather_kernel(rows, chans, halves_of, *refs)

    def several(lead, x):
        return jax.ShapeDtypeStruct(lead + x.shape, x.dtype)

    return pl.pallas_call(
        kernel,
        out_shape=(
            several((3,), za_cols),
            several((), zb_cols),
            several((chans,), w_in),
            several((chans,), w_out),
            several((chans,), bias),
        ),
        in_specs=[vmem] * 5,
        out_specs=(vmem,) * 5,
        scratch_shapes=[
            pltpu.SemaphoreType.DMA((2, 3 * chans)),
            pltpu.SemaphoreType.DMA((2, 2, chans)),
            pltpu.SemaphoreType.DMA((2, 2, 3)),
            pltpu.SemaphoreType.DMA((2, 2, 3)),
            pltpu.SemaphoreType.DMA((5,)),
        ],
        compiler_params=pltpu.CompilerParams(collective_id=0, has_side_effects=True),
        name="gather_inputs",
    )(za_cols, zb_cols, w_in, w_out, bias)


def as_column(line):
    size = line.shape[1]
    down = lax.broadcasted_iota(jnp.int32, (size, size), 0)
    along = lax.broadcasted_iota(jnp.int32, (size, size), 1)
    return jnp.sum(jnp.where(down == along, line, 0.0), axis=1, keepdims=True)


def couple_kernel(dims, refs, taps_ref, hidden_ref):
    slab, half, quarter, hidden_local, groups, block, width, height = dims
    za_ref, zb_ref, win_ref, wout_ref, bias_ref, bout_ref, unmix_ref, out_ref = refs
    wide = za_ref.shape[2]
    first_row = lax.axis_index("rows") * slab - slab
    first_col = lax.axis_index("chan") * block - 1
    span = 3 * half
    for row in range(3 * slab):
        plane = za_ref[row].astype(jnp.float32)
        for off in range(3):
            moved = plane if off == 0 else pltpu.roll(plane, wide - off, 1)
            taps_ref[pl.ds(row * span + off * half, half), :] = moved.astype(jnp.bfloat16)
    cols = first_col + lax.broadcasted_iota(jnp.int32, (hidden_local, wide), 1)
    inside = (cols >= 0) & (cols < width)
    deep = 3 * hidden_local
    biases = [as_column(bias_ref[part]) for part in range(groups)]
    out_bias = as_column(bout_ref[...])
    for row in range(2 * slab):
        line = first_row + row + 1
        keep = inside & (line >= 0) & (line < height)
        stack = taps_ref[pl.ds(row * span, 3 * span), :]
        for part in range(groups):
            value = lax.dot_general(
                win_ref[part], stack, (((1,), (0,)), ((), ())), preferred_element_type=jnp.float32
            )
            value = jnp.maximum(value + biases[part], 0.0)
            value = jnp.where(keep, value, 0.0)
            for off in range(3):
                moved = value if off == 0 else pltpu.roll(value, wide - off, 1)
                hidden_ref[part, pl.ds(row * deep + off * hidden_local, hidden_local), :] = moved[
                    :, :block
                ].astype(jnp.bfloat16)
    share = unmix_ref.shape[0] // groups
    for row in range(slab):
        raw = out_bias + jnp.zeros((2 * half, block), jnp.float32)
        for part in range(groups):
            raw = raw + jnp.dot(
                wout_ref[part],
                hidden_ref[part, pl.ds(row * deep, 3 * deep), :],
                preferred_element_type=jnp.float32,
            )
        latent = zb_ref[row].astype(jnp.float32)
        coupled = (latent - raw[half:]) * jnp.exp(-jnp.tanh(raw[:half]))
        own = pltpu.roll(za_ref[slab + row].astype(jnp.float32), wide - 2, 1)[:, :block]
        joined = jnp.concatenate([own, coupled], axis=0)
        mixed = jnp.dot(
            unmix_ref[...],
            joined,
            precision=lax.Precision.HIGHEST,
            preferred_element_type=jnp.float32,
        )
        for part in range(groups):
            out_ref[part, pl.ds(row * share, share), :] = mixed[part * share : (part + 1) * share]


def split(values):
    high = values.astype(jnp.bfloat16)
    return high, (values - high.astype(jnp.float32)).astype(jnp.bfloat16)


def main_kernel(dims, counts, *refs):
    slab, half, quarter, hidden_local, groups, block, width, height = dims
    rows, triple, lanes = counts
    couple_refs = refs[:7]
    thigh_ref, tlow_ref, fhigh_ref, flow_ref, bhigh_ref, blow_ref = refs[7:13]
    near_ref, turn_ref, lane_ref, out_ref = refs[13:17]
    taps_ref, hidden_ref, mix_ref, mixed_ref, send_ref, got_ref, back_ref, home_ref = refs[17:25]
    work_ref, own_sem, chan_sem, there_sem, back_sem = refs[25:]
    mine = 2 * half // groups
    tile = 2 * lanes
    freq_groups = width // lanes
    chan_groups = rows // freq_groups
    me_row = lax.axis_index("rows")
    me_chan = lax.axis_index("chan")
    barrier = pltpu.get_barrier_semaphore()

    def greet(step, carry):
        pl.semaphore_signal(
            barrier,
            inc=1,
            device_id=(lax.rem(me_row + step, rows), me_chan),
            device_id_type=mesh_ids,
        )
        return carry

    for step in range(1, groups):
        pl.semaphore_signal(
            barrier,
            inc=1,
            device_id=(me_row, lax.rem(me_chan + step, groups)),
            device_id_type=mesh_ids,
        )
    lax.fori_loop(1, rows, greet, 0)
    couple_kernel(dims, tuple(couple_refs) + (mix_ref,), taps_ref, hidden_ref)
    pl.semaphore_wait(barrier, rows - 1 + groups - 1)

    swaps = []
    for step in range(1, groups):
        peer = lax.rem(me_chan + step, groups)
        swaps.append(
            pltpu.make_async_remote_copy(
                src_ref=mix_ref.at[peer],
                dst_ref=mixed_ref.at[me_chan],
                send_sem=chan_sem.at[0, step],
                recv_sem=chan_sem.at[1, step],
                device_id=(me_row, peer),
                device_id_type=mesh_ids,
            )
        )
    for one in swaps:
        one.start()
    own = pltpu.make_async_copy(mix_ref.at[me_chan], mixed_ref.at[me_chan], own_sem.at[0])
    own.start()
    own.wait()
    for one in swaps:
        one.wait()

    high, low = split(jnp.concatenate([mixed_ref[i] for i in range(groups)], axis=1))
    lead = slab * mine
    both = jnp.dot(
        jnp.concatenate([high, low], axis=0), thigh_ref[...], preferred_element_type=jnp.float32
    )
    packed = both[:lead] + both[lead:]
    packed = packed + jnp.dot(high, tlow_ref[...], preferred_element_type=jnp.float32)
    lane = lax.broadcasted_iota(jnp.int32, (mine, tile), 1)
    for pair in range(freq_groups // 2):
        first = packed[:mine, pair * tile : (pair + 1) * tile]
        second = packed[mine:, pair * tile : (pair + 1) * tile]
        even = jnp.where(lane < lanes, first, pltpu.roll(second, lanes, 1))
        odd = jnp.where(lane < lanes, pltpu.roll(first, lanes, 1), second)
        for which, value in ((2 * pair, even), (2 * pair + 1, odd)):
            for group in range(chan_groups):
                send_ref[which * chan_groups + group] = value[
                    group * triple : (group + 1) * triple
                ]

    def exchange(source, target, sems, own_at):
        def copy(step):
            peer = lax.rem(me_row + step, rows)
            return pltpu.make_async_remote_copy(
                src_ref=source.at[peer],
                dst_ref=target.at[me_row],
                send_sem=sems.at[0, step],
                recv_sem=sems.at[1, step],
                device_id=(peer, me_chan),
                device_id_type=mesh_ids,
            )

        def start(step, carry):
            copy(step).start()
            return carry

        def finish(step, carry):
            copy(step).wait()
            return carry

        lax.fori_loop(1, rows, start, 0)
        kept = pltpu.make_async_copy(source.at[me_row], target.at[me_row], own_sem.at[own_at])
        kept.start()
        kept.wait()
        lax.fori_loop(1, rows, finish, 0)

    exchange(send_ref, got_ref, there_sem, 1)

    lane = lax.broadcasted_iota(jnp.int32, (rows, tile), 1)
    sign = lane_ref[pl.ds(0, 1), :]
    scale = lane_ref[pl.ds(1, 1), :]
    stacks = []
    for chan in range(triple):
        data = got_ref[:, chan, :]
        other = jnp.where(
            lax.rem(lane, lanes) < lanes // 2,
            pltpu.roll(data, tile - lanes // 2, 1),
            pltpu.roll(data, lanes // 2, 1),
        )
        stacks.append(jnp.concatenate([data, other * sign], axis=0))
    high, low = split(jnp.concatenate(stacks, axis=1))
    forward = jnp.dot(fhigh_ref[...], high, preferred_element_type=jnp.float32)
    forward = forward + jnp.dot(fhigh_ref[...], low, preferred_element_type=jnp.float32)
    forward = forward + jnp.dot(flow_ref[...], high, preferred_element_type=jnp.float32)
    cos_u = turn_ref[0]
    sin_u = turn_ref[1]
    solved = []
    for chan in range(triple):
        piece = forward[:, chan * tile : (chan + 1) * tile]
        parts = [piece[i * height : (i + 1) * height] for i in range(4)]
        real_part = parts[0] + pltpu.roll(parts[1], lanes, 1)
        imag_part = parts[2] + pltpu.roll(parts[3], lanes, 1)
        near = [near_ref[i, pl.ds(chan, 1), :] for i in range(6)]
        symbol_real = near[1] + (near[0] + near[2]) * cos_u + (near[3] - near[5]) * sin_u
        symbol_imag = near[4] + (near[3] + near[5]) * cos_u + (near[2] - near[0]) * sin_u
        factor = scale / (symbol_real * symbol_real + symbol_imag * symbol_imag)
        solved.append(
            jnp.concatenate(
                [
                    (real_part * symbol_real + imag_part * symbol_imag) * factor,
                    (imag_part * symbol_real - real_part * symbol_imag) * factor,
                ],
                axis=0,
            )
        )
    high, low = split(jnp.concatenate(solved, axis=1))
    inverse = jnp.dot(bhigh_ref[...], high, preferred_element_type=jnp.float32)
    inverse = inverse + jnp.dot(bhigh_ref[...], low, preferred_element_type=jnp.float32)
    inverse = inverse + jnp.dot(blow_ref[...], high, preferred_element_type=jnp.float32)
    for chan in range(triple):
        piece = inverse[:, chan * tile : (chan + 1) * tile]
        back_ref[:, chan, :] = jnp.where(
            lane < lanes, piece[:rows], pltpu.roll(piece[rows:], lanes, 1)
        )

    exchange(back_ref, home_ref, back_sem, 2)

    for which in range(rows):
        work_ref[which // chan_groups, pl.ds(which % chan_groups * triple, triple), :] = home_ref[
            which
        ]
    lane = lax.broadcasted_iota(jnp.int32, (mine, tile), 1)
    upper = []
    lower = []
    for pair in range(freq_groups // 2):
        even = work_ref[2 * pair]
        odd = work_ref[2 * pair + 1]
        upper.append(jnp.where(lane < lanes, even, pltpu.roll(odd, lanes, 1)))
        lower.append(jnp.where(lane < lanes, pltpu.roll(even, lanes, 1), odd))
    final = jnp.concatenate(
        [jnp.concatenate(upper, axis=1), jnp.concatenate(lower, axis=1)], axis=0
    )
    high, low = split(final)

    def across(values, table):
        return lax.dot_general(
            values, table[...], (((1,), (1,)), ((), ())), preferred_element_type=jnp.float32
        )

    both = across(jnp.concatenate([high, low], axis=0), thigh_ref)
    result = both[:lead] + both[lead:] + across(high, tlow_ref)
    for row in range(slab):
        out_ref[row] = result[row * mine : (row + 1) * mine]


def whole(operands, dims, counts):
    slab, half, quarter, hidden_local, groups, block, width, height = dims
    rows, triple, lanes = counts
    wide = operands[0].shape[2]
    mine = 2 * half // groups
    tile = 2 * lanes

    def kernel(*refs):
        main_kernel(dims, counts, *refs)

    mix = pltpu.VMEM((groups, slab * mine, block), jnp.float32)
    message = pltpu.VMEM((rows, triple, tile), jnp.float32)
    return pl.pallas_call(
        kernel,
        out_shape=jax.ShapeDtypeStruct((slab, mine, width), jnp.float32),
        in_specs=[vmem] * len(operands),
        out_specs=vmem,
        scratch_shapes=[
            pltpu.VMEM((3 * slab * 3 * half, wide), jnp.bfloat16),
            pltpu.VMEM((groups, 2 * slab * 3 * hidden_local, block), jnp.bfloat16),
            mix,
            mix,
            message,
            message,
            message,
            message,
            pltpu.VMEM((width // lanes, mine, tile), jnp.float32),
            pltpu.SemaphoreType.DMA((3,)),
            pltpu.SemaphoreType.DMA((2, groups)),
            pltpu.SemaphoreType.DMA((2, rows)),
            pltpu.SemaphoreType.DMA((2, rows)),
        ],
        compiler_params=pltpu.CompilerParams(collective_id=1, has_side_effects=True),
        name="couple_and_solve",
    )(*operands)


def halves(values):
    high = lax.reduce_precision(values, 8, 7)
    return high.astype(jnp.bfloat16), (values - high).astype(jnp.bfloat16)


def column_tables(width, group):
    pos = np.arange(width)
    part = pos // group % 2
    slot = pos // (2 * group) * group + pos % group
    first = slot == 0
    freq = np.where(first & (part == 1), width // 2, slot)
    shift = np.where(first, 0, part) * (math.pi / 2)
    fine = 32
    outer = (np.arange(width // fine) * fine)[:, None] * freq[None, :] % width * (full_turn / width)
    inner = np.arange(fine)[:, None] * freq[None, :] % width * (full_turn / width) + shift[None, :]
    consts = [f(a).astype(np.float32) for a in (outer, inner) for f in (np.cos, np.sin)]
    cos_o, sin_o, cos_i, sin_i = lax.optimization_barrier(tuple(jnp.asarray(c) for c in consts))
    table = cos_o[:, None, :] * cos_i[None] - sin_o[:, None, :] * sin_i[None]
    table = table.reshape(width, width)
    sign = np.where(first, 0.0, 1.0 - 2.0 * part).astype(np.float32)
    weight = np.where(first, 1.0, 2.0).astype(np.float32)
    return halves(table), freq, sign, weight


def on_device(za, zb, w_in, b_in, w_out, b_out, unmix, kern):
    slab, quarter, width = za.shape
    hidden_local = w_in.shape[3]
    chans = unmix.shape[0]
    half = chans // 2
    rows = lax.axis_size("rows")
    groups = lax.axis_size("chan")
    row_idx = lax.axis_index("rows")
    chan_idx = lax.axis_index("chan")
    height = slab * rows
    block = width // groups
    mine = chans // groups
    lanes = 64
    freq_groups = width // lanes
    chan_groups = rows // freq_groups
    triple = mine // chan_groups

    table, freq, sign, weight = column_tables(width, lanes // 2)

    zb_cols = zb.reshape(slab * quarter, groups, block).transpose(1, 0, 2)
    za_wide = jnp.pad(za.reshape(slab * quarter, width), ((0, 0), (2, 128 + 2)))
    za_cols = jnp.stack(
        [za_wide[:, block * i : block * i + block + 128] for i in range(groups)], axis=0
    )
    taps = 9
    w_in_parts = w_in.reshape(taps * half, hidden_local).T.reshape(
        2, hidden_local // 2, taps * half
    )
    w_out_parts = w_out.reshape(taps * hidden_local, chans).T.reshape(
        2, chans // 2, taps * hidden_local
    )
    za_got, zb_got, w_in_all, w_out_all, bias = gather(
        za_cols, zb_cols, w_in_parts, w_out_parts, b_in[None, :], rows, groups, 2
    )
    za_ext = za_got.reshape(3, groups, slab, quarter, block + 128)
    za_ext = za_ext.transpose(0, 2, 1, 3, 4).reshape(3 * slab, half, block + 128)
    ext_rows = row_idx * slab - slab + jnp.arange(3 * slab, dtype=jnp.int32)
    inside = (ext_rows >= 0) & (ext_rows < height)
    za_ext = jnp.where(inside[:, None, None], za_ext, jnp.zeros((), za.dtype))
    latent = zb_got.reshape(groups, slab, quarter, block).transpose(1, 0, 2, 3)
    freq_idx = row_idx // chan_groups
    chan_first = chan_idx * mine + row_idx % chan_groups * triple
    turn = freq * (full_turn / width)
    lane_rows = np.stack([sign, weight * (1.0 / (height * width)), np.cos(turn), np.sin(turn)])
    lane_rows = lane_rows.astype(np.float32).reshape(4, freq_groups, lanes).transpose(1, 0, 2)
    lane_rows = np.concatenate([lane_rows, lane_rows], axis=2)
    lane_own = lax.dynamic_index_in_dim(jnp.asarray(lane_rows), freq_idx, 0, keepdims=False)
    cos_v = lane_own[2][None, None, :]
    sin_v = lane_own[3][None, None, :]
    stencil = lax.dynamic_slice_in_dim(kern, chan_first, triple, 2)[..., None]
    near_real = stencil[:, 1] + (stencil[:, 0] + stencil[:, 2]) * cos_v
    near_imag = (stencil[:, 2] - stencil[:, 0]) * sin_v
    near = jnp.concatenate([near_real, near_imag], axis=0)
    row_turn = np.arange(height) * (full_turn / height)
    turns = np.stack([np.cos(row_turn), np.sin(row_turn)]).astype(np.float32)
    turns = np.broadcast_to(turns[:, :, None], (2, height, 2 * lanes))

    blocks = []
    for row in range(slab):
        order = np.arange(rows) * slab + row
        angles = np.arange(height)[:, None] * order[None, :] % height * (full_turn / height)
        blocks.append((np.cos(angles), np.sin(angles)))
    ahead = [np.concatenate([c, t], axis=1) for c, t in blocks]
    ahead += [np.concatenate([-t, c], axis=1) for c, t in blocks]
    behind = [np.concatenate([c.T, -t.T], axis=1) for c, t in blocks]

    def fixed(pieces):
        values = np.concatenate(pieces, axis=0)
        high = values.astype(jnp.bfloat16)
        low = (values - high.astype(np.float64)).astype(jnp.bfloat16)
        return jnp.asarray(high), jnp.asarray(low)

    operands = (
        za_ext,
        latent.reshape(slab, half, block),
        w_in_all.reshape(groups, hidden_local, taps * half),
        w_out_all.reshape(groups, chans, taps * hidden_local),
        bias,
        b_out.reshape(1, chans),
        unmix,
        *table,
        *fixed(ahead),
        *fixed(behind),
        near,
        jnp.asarray(turns),
        lane_own,
    )
    dims = (slab, half, quarter, hidden_local, groups, block, width, height)
    return whole(operands, dims, (rows, triple, lanes))


def solution(mesh):
    placed = (
        P("rows", "chan", None),
        P("rows", "chan", None),
        P(None, None, None, "chan"),
        P("chan"),
        P(None, None, "chan", None, None),
        P(),
        P(),
        P(),
    )
    return jax.shard_map(
        on_device, mesh=mesh, in_specs=placed, out_specs=P("rows", "chan", None), check_vma=False
    )
```

```python
import math

import jax
import jax.numpy as jnp
import numpy as np
from jax import lax
from jax.experimental import pallas as pl
from jax.experimental.pallas import tpu as pltpu
from jax.sharding import PartitionSpec as P

full_turn = 2.0 * math.pi
vmem = pl.BlockSpec(memory_space=pltpu.VMEM)
mesh_ids = pl.DeviceIdType.MESH


def split(values):
    high = values.astype(jnp.bfloat16)
    return high, (values - high.astype(jnp.float32)).astype(jnp.bfloat16)


def gather_kernel(rows, chans, halves_of, *refs):
    za_ref, zb_ref, win_ref, wout_ref, bias_ref, turn_ref = refs[:6]
    za_out, zb_out, win_out, wout_out, bias_out, high_out, low_out = refs[6:13]
    za_sems, zb_sems, w_sems, pass_sems, own_sem = refs[13:]
    me_row = lax.axis_index("rows")
    me_chan = lax.axis_index("chan")
    core = lax.rem(me_row, 2)
    side = lax.rem(me_row // 2, halves_of)
    ring = halves_of * chans
    spot = side * chans + me_chan
    partner = (me_row + 1 - 2 * core, me_chan)
    barrier = pltpu.get_barrier_semaphore()
    peers = [(dr, dc) for dr in (0, 1, 2) for dc in range(chans) if (dr, dc) != (1, 0)]
    steps = (1, ring - 1, 2 + core * (ring - 4))

    def place(dr, dc):
        return (lax.rem(me_row + dr + rows - 1, rows), lax.rem(me_chan + dc, chans))

    def around(step):
        there = lax.rem(spot + step, ring)
        return (me_row + (there // chans - side) * 2, lax.rem(there, chans))

    for step in steps:
        pl.semaphore_signal(
            barrier, inc=1, device_id=around(ring - step), device_id_type=mesh_ids
        )
    for dr, dc in peers:
        pl.semaphore_signal(barrier, inc=1, device_id=place(dr, dc), device_id_type=mesh_ids)
    own = [
        pltpu.make_async_copy(win_ref, win_out.at[me_chan], own_sem.at[0]),
        pltpu.make_async_copy(wout_ref, wout_out.at[me_chan], own_sem.at[1]),
        pltpu.make_async_copy(za_ref.at[me_chan], za_out.at[1, me_chan], own_sem.at[2]),
        pltpu.make_async_copy(zb_ref.at[me_chan], zb_out.at[me_chan], own_sem.at[3]),
        pltpu.make_async_copy(bias_ref, bias_out.at[me_chan], own_sem.at[4]),
    ]
    for one in own:
        one.start()
    pl.semaphore_wait(barrier, len(peers) + len(steps))
    first = []
    for idx, step in enumerate(steps):
        for kind, (source, target) in enumerate(((wout_ref, wout_out), (win_ref, win_out))):
            first.append(
                pltpu.make_async_remote_copy(
                    src_ref=source.at[core],
                    dst_ref=target.at[me_chan, core],
                    send_sem=w_sems.at[0, kind, idx],
                    recv_sem=w_sems.at[1, kind, idx],
                    device_id=around(step),
                    device_id_type=mesh_ids,
                )
            )
    copies = []
    for idx, (dr, dc) in enumerate(peers):
        there = place(dr, dc)
        copies.append(
            pltpu.make_async_remote_copy(
                src_ref=za_ref.at[there[1]],
                dst_ref=za_out.at[2 - dr, me_chan],
                send_sem=za_sems.at[0, idx],
                recv_sem=za_sems.at[1, idx],
                device_id=there,
                device_id_type=mesh_ids,
            )
        )
    for dc in range(1, chans):
        peer = lax.rem(me_chan + dc, chans)
        pairs = ((zb_ref.at[peer], zb_out), (bias_ref, bias_out))
        for kind, (source, target) in enumerate(pairs):
            copies.append(
                pltpu.make_async_remote_copy(
                    src_ref=source,
                    dst_ref=target.at[me_chan],
                    send_sem=zb_sems.at[0, kind, dc],
                    recv_sem=zb_sems.at[1, kind, dc],
                    device_id=(me_row, peer),
                    device_id_type=mesh_ids,
                )
            )
    for one in first:
        one.start()
    for one in copies:
        one.start()
    fine = turn_ref.shape[1]

    def fill(outer, carry):
        at = pl.ds(outer, 1)
        values = turn_ref[0, at, :] * turn_ref[2] - turn_ref[1, at, :] * turn_ref[3]
        high, low = split(values)
        here = pl.ds(pl.multiple_of(outer * fine, fine), fine)
        high_out[here, :] = high
        low_out[here, :] = low
        return carry

    lax.fori_loop(0, high_out.shape[0] // fine, fill, 0)
    passed = []
    for idx, step in enumerate(steps):
        origin = lax.rem(spot + ring - step, ring)
        quarter = lax.rem(origin, chans)
        for kind, target in enumerate((wout_out, win_out)):
            first[2 * idx + kind].wait_recv()
            one = pltpu.make_async_remote_copy(
                src_ref=target.at[quarter, core],
                dst_ref=target.at[quarter, core],
                send_sem=pass_sems.at[0, kind, idx],
                recv_sem=pass_sems.at[1, kind, idx],
                device_id=partner,
                device_id_type=mesh_ids,
            )
            one.start()
            passed.append(one)
    for one in own:
        one.wait()
    for one in copies:
        one.wait()
    for one in passed:
        one.wait()
    for one in first:
        one.wait_send()


def gather(za_cols, zb_cols, w_in, w_out, bias, turns, rows, chans, halves_of):
    def kernel(*refs):
        gather_kernel(rows, chans, halves_of, *refs)

    def several(lead, x):
        return jax.ShapeDtypeStruct(lead + x.shape, x.dtype)

    return pl.pallas_call(
        kernel,
        out_shape=(
            several((3,), za_cols),
            several((), zb_cols),
            several((chans,), w_in),
            several((chans,), w_out),
            several((chans,), bias),
            jax.ShapeDtypeStruct((turns.shape[2],) * 2, jnp.bfloat16),
            jax.ShapeDtypeStruct((turns.shape[2],) * 2, jnp.bfloat16),
        ),
        in_specs=[vmem] * 6,
        out_specs=(vmem,) * 7,
        scratch_shapes=[
            pltpu.SemaphoreType.DMA((2, 3 * chans)),
            pltpu.SemaphoreType.DMA((2, 2, chans)),
            pltpu.SemaphoreType.DMA((2, 2, 3)),
            pltpu.SemaphoreType.DMA((2, 2, 3)),
            pltpu.SemaphoreType.DMA((5,)),
        ],
        compiler_params=pltpu.CompilerParams(collective_id=0, has_side_effects=True),
        name="gather_inputs",
    )(za_cols, zb_cols, w_in, w_out, bias, turns)


def as_column(line):
    size = line.shape[1]
    down = lax.broadcasted_iota(jnp.int32, (size, size), 0)
    along = lax.broadcasted_iota(jnp.int32, (size, size), 1)
    return jnp.sum(jnp.where(down == along, line, 0.0), axis=1, keepdims=True)


def couple_kernel(dims, refs, plane_ref, latent_ref, taps_ref, hidden_ref):
    slab, half, quarter, hidden_local, groups, block, width, height = dims
    za_ref, zb_ref, win_ref, wout_ref, bias_ref, bout_ref, unmix_ref, out_ref = refs
    wide = za_ref.shape[3]
    first_row = lax.axis_index("rows") * slab - slab
    first_col = lax.axis_index("chan") * block - 1
    span = 3 * half
    for row in range(3 * slab):
        line = first_row + row
        held = (line >= 0) & (line < height)
        for part in range(groups):
            piece = za_ref[row // slab, part].astype(jnp.float32)
            piece = piece[row % slab * quarter : (row % slab + 1) * quarter]
            plane_ref[row, pl.ds(part * quarter, quarter), :] = jnp.where(held, piece, 0.0)
        plane = plane_ref[row]
        for off in range(3):
            moved = plane if off == 0 else pltpu.roll(plane, wide - off, 1)
            taps_ref[pl.ds(row * span + off * half, half), :] = moved.astype(jnp.bfloat16)
    cols = first_col + lax.broadcasted_iota(jnp.int32, (hidden_local, wide), 1)
    inside = (cols >= 0) & (cols < width)
    deep = 3 * hidden_local
    biases = [as_column(bias_ref[part]) for part in range(groups)]
    out_bias = jnp.concatenate([as_column(bout_ref[pl.ds(i, 1), :]) for i in range(2)], axis=0)
    for row in range(2 * slab):
        line = first_row + row + 1
        keep = inside & (line >= 0) & (line < height)
        stack = taps_ref[pl.ds(row * span, 3 * span), :]
        for part in range(groups):
            value = lax.dot_general(
                win_ref[part], stack, (((1,), (0,)), ((), ())), preferred_element_type=jnp.float32
            )
            value = jnp.maximum(value + biases[part], 0.0)
            value = jnp.where(keep, value, 0.0)
            for off in range(3):
                moved = value if off == 0 else pltpu.roll(value, wide - off, 1)
                hidden_ref[part, pl.ds(row * deep + off * hidden_local, hidden_local), :] = moved[
                    :, :block
                ].astype(jnp.bfloat16)
    share = unmix_ref.shape[0] // groups
    for row in range(slab):
        raw = out_bias + jnp.zeros((2 * half, block), jnp.float32)
        for part in range(groups):
            raw = raw + jnp.dot(
                wout_ref[part],
                hidden_ref[part, pl.ds(row * deep, 3 * deep), :],
                preferred_element_type=jnp.float32,
            )
        for part in range(groups):
            piece = zb_ref[part].astype(jnp.float32)[row * quarter : (row + 1) * quarter]
            latent_ref[row, pl.ds(part * quarter, quarter), :] = piece
        latent = latent_ref[row]
        coupled = (latent - raw[half:]) * jnp.exp(-jnp.tanh(raw[:half]))
        own = pltpu.roll(plane_ref[slab + row], wide - 2, 1)[:, :block]
        joined = jnp.concatenate([own, coupled], axis=0)
        mixed = jnp.dot(
            unmix_ref[...],
            joined,
            precision=lax.Precision.HIGHEST,
            preferred_element_type=jnp.float32,
        )
        for part in range(groups):
            out_ref[part, pl.ds(row * share, share), :] = mixed[part * share : (part + 1) * share]


def main_kernel(dims, counts, *refs):
    slab, half, quarter, hidden_local, groups, block, width, height = dims
    rows, triple, lanes = counts
    couple_refs = refs[:7]
    thigh_ref, tlow_ref, fhigh_ref, flow_ref, bhigh_ref, blow_ref = refs[7:13]
    kern_ref, turn_ref, lane_ref, out_ref = refs[13:17]
    plane_ref, latent_ref, taps_ref, hidden_ref, kern_cols = refs[17:22]
    mix_ref, mixed_ref, send_ref, got_ref, back_ref, home_ref = refs[22:28]
    work_ref, own_sem, chan_sem, there_sem, back_sem = refs[28:]
    mine = 2 * half // groups
    tile = 2 * lanes
    freq_groups = width // lanes
    chan_groups = rows // freq_groups
    me_row = lax.axis_index("rows")
    me_chan = lax.axis_index("chan")
    barrier = pltpu.get_barrier_semaphore()

    def greet(step, carry):
        pl.semaphore_signal(
            barrier,
            inc=1,
            device_id=(lax.rem(me_row + step, rows), me_chan),
            device_id_type=mesh_ids,
        )
        return carry

    for step in range(1, groups):
        pl.semaphore_signal(
            barrier,
            inc=1,
            device_id=(me_row, lax.rem(me_chan + step, groups)),
            device_id_type=mesh_ids,
        )
    lax.fori_loop(1, rows, greet, 0)
    couple_kernel(
        dims, tuple(couple_refs) + (mix_ref,), plane_ref, latent_ref, taps_ref, hidden_ref
    )
    at = lax.broadcasted_iota(jnp.int32, kern_cols.shape, 1)
    spread = jnp.zeros(kern_cols.shape, jnp.float32)
    for row_off in range(3):
        for col_off in range(3):
            column = as_column(kern_ref[row_off, pl.ds(col_off, 1), :])
            spread = jnp.where(at == 3 * row_off + col_off, column, spread)
    kern_cols[...] = spread
    pl.semaphore_wait(barrier, rows - 1 + groups - 1)

    swaps = []
    for step in range(1, groups):
        peer = lax.rem(me_chan + step, groups)
        swaps.append(
            pltpu.make_async_remote_copy(
                src_ref=mix_ref.at[peer],
                dst_ref=mixed_ref.at[me_chan],
                send_sem=chan_sem.at[0, step],
                recv_sem=chan_sem.at[1, step],
                device_id=(me_row, peer),
                device_id_type=mesh_ids,
            )
        )
    for one in swaps:
        one.start()
    own = pltpu.make_async_copy(mix_ref.at[me_chan], mixed_ref.at[me_chan], own_sem.at[0])
    own.start()
    own.wait()
    for one in swaps:
        one.wait()

    high, low = split(jnp.concatenate([mixed_ref[i] for i in range(groups)], axis=1))
    lead = slab * mine
    both = jnp.dot(
        jnp.concatenate([high, low], axis=0), thigh_ref[...], preferred_element_type=jnp.float32
    )
    packed = both[:lead] + both[lead:]
    packed = packed + jnp.dot(high, tlow_ref[...], preferred_element_type=jnp.float32)
    lane = lax.broadcasted_iota(jnp.int32, (mine, tile), 1)
    for pair in range(freq_groups // 2):
        first = packed[:mine, pair * tile : (pair + 1) * tile]
        second = packed[mine:, pair * tile : (pair + 1) * tile]
        even = jnp.where(lane < lanes, first, pltpu.roll(second, lanes, 1))
        odd = jnp.where(lane < lanes, pltpu.roll(first, lanes, 1), second)
        for which, value in ((2 * pair, even), (2 * pair + 1, odd)):
            for group in range(chan_groups):
                send_ref[which * chan_groups + group] = value[
                    group * triple : (group + 1) * triple
                ]

    def exchange(source, target, sems, own_at):
        def copy(step):
            peer = lax.rem(me_row + step, rows)
            return pltpu.make_async_remote_copy(
                src_ref=source.at[peer],
                dst_ref=target.at[me_row],
                send_sem=sems.at[0, step],
                recv_sem=sems.at[1, step],
                device_id=(peer, me_chan),
                device_id_type=mesh_ids,
            )

        def start(step, carry):
            copy(step).start()
            return carry

        def finish(step, carry):
            copy(step).wait()
            return carry

        lax.fori_loop(1, rows, start, 0)
        kept = pltpu.make_async_copy(source.at[me_row], target.at[me_row], own_sem.at[own_at])
        kept.start()
        kept.wait()
        lax.fori_loop(1, rows, finish, 0)

    exchange(send_ref, got_ref, there_sem, 1)

    lane = lax.broadcasted_iota(jnp.int32, (rows, tile), 1)
    lane_table = lane_ref[me_row // chan_groups]
    sign = lane_table[0:1]
    scale = lane_table[1:2]
    cos_v = lane_table[2:3]
    sin_v = lane_table[3:4]
    chan_first = me_chan * mine + lax.rem(me_row, chan_groups) * triple
    stacks = []
    for chan in range(triple):
        data = got_ref[:, chan, :]
        other = jnp.where(
            lax.rem(lane, lanes) < lanes // 2,
            pltpu.roll(data, tile - lanes // 2, 1),
            pltpu.roll(data, lanes // 2, 1),
        )
        stacks.append(jnp.concatenate([data, other * sign], axis=0))
    high, low = split(jnp.concatenate(stacks, axis=1))
    forward = jnp.dot(fhigh_ref[...], high, preferred_element_type=jnp.float32)
    forward = forward + jnp.dot(fhigh_ref[...], low, preferred_element_type=jnp.float32)
    forward = forward + jnp.dot(flow_ref[...], high, preferred_element_type=jnp.float32)
    cos_u = as_column(turn_ref[pl.ds(0, 1), :])
    sin_u = as_column(turn_ref[pl.ds(1, 1), :])
    solved = []
    for chan in range(triple):
        piece = forward[:, chan * tile : (chan + 1) * tile]
        parts = [piece[i * height : (i + 1) * height] for i in range(4)]
        real_part = parts[0] + pltpu.roll(parts[1], lanes, 1)
        imag_part = parts[2] + pltpu.roll(parts[3], lanes, 1)
        stencil = kern_cols[pl.ds(chan_first + chan, 1), :]
        taps = [stencil[:, i : i + 1] for i in range(9)]
        near = [taps[3 * i + 1] + (taps[3 * i] + taps[3 * i + 2]) * cos_v for i in range(3)]
        near += [(taps[3 * i + 2] - taps[3 * i]) * sin_v for i in range(3)]
        symbol_real = near[1] + (near[0] + near[2]) * cos_u + (near[3] - near[5]) * sin_u
        symbol_imag = near[4] + (near[3] + near[5]) * cos_u + (near[2] - near[0]) * sin_u
        factor = scale / (symbol_real * symbol_real + symbol_imag * symbol_imag)
        solved.append(
            jnp.concatenate(
                [
                    (real_part * symbol_real + imag_part * symbol_imag) * factor,
                    (imag_part * symbol_real - real_part * symbol_imag) * factor,
                ],
                axis=0,
            )
        )
    high, low = split(jnp.concatenate(solved, axis=1))
    inverse = jnp.dot(bhigh_ref[...], high, preferred_element_type=jnp.float32)
    inverse = inverse + jnp.dot(bhigh_ref[...], low, preferred_element_type=jnp.float32)
    inverse = inverse + jnp.dot(blow_ref[...], high, preferred_element_type=jnp.float32)
    for chan in range(triple):
        piece = inverse[:, chan * tile : (chan + 1) * tile]
        back_ref[:, chan, :] = jnp.where(
            lane < lanes, piece[:rows], pltpu.roll(piece[rows:], lanes, 1)
        )

    exchange(back_ref, home_ref, back_sem, 2)

    for which in range(rows):
        work_ref[which // chan_groups, pl.ds(which % chan_groups * triple, triple), :] = home_ref[
            which
        ]
    lane = lax.broadcasted_iota(jnp.int32, (mine, tile), 1)
    upper = []
    lower = []
    for pair in range(freq_groups // 2):
        even = work_ref[2 * pair]
        odd = work_ref[2 * pair + 1]
        upper.append(jnp.where(lane < lanes, even, pltpu.roll(odd, lanes, 1)))
        lower.append(jnp.where(lane < lanes, pltpu.roll(even, lanes, 1), odd))
    final = jnp.concatenate(
        [jnp.concatenate(upper, axis=1), jnp.concatenate(lower, axis=1)], axis=0
    )
    high, low = split(final)

    def across(values, table):
        return lax.dot_general(
            values, table[...], (((1,), (1,)), ((), ())), preferred_element_type=jnp.float32
        )

    both = across(jnp.concatenate([high, low], axis=0), thigh_ref)
    result = both[:lead] + both[lead:] + across(high, tlow_ref)
    for row in range(slab):
        out_ref[row] = result[row * mine : (row + 1) * mine]


def whole(operands, dims, counts):
    slab, half, quarter, hidden_local, groups, block, width, height = dims
    rows, triple, lanes = counts
    wide = operands[0].shape[3]
    mine = 2 * half // groups
    tile = 2 * lanes

    def kernel(*refs):
        main_kernel(dims, counts, *refs)

    mix = pltpu.VMEM((groups, slab * mine, block), jnp.float32)
    message = pltpu.VMEM((rows, triple, tile), jnp.float32)
    return pl.pallas_call(
        kernel,
        out_shape=jax.ShapeDtypeStruct((slab, mine, width), jnp.float32),
        in_specs=[vmem] * len(operands),
        out_specs=vmem,
        scratch_shapes=[
            pltpu.VMEM((3 * slab, half, wide), jnp.float32),
            pltpu.VMEM((slab, half, block), jnp.float32),
            pltpu.VMEM((3 * slab * 3 * half, wide), jnp.bfloat16),
            pltpu.VMEM((groups, 2 * slab * 3 * hidden_local, block), jnp.bfloat16),
            pltpu.VMEM((2 * half, tile), jnp.float32),
            mix,
            mix,
            message,
            message,
            message,
            message,
            pltpu.VMEM((width // lanes, mine, tile), jnp.float32),
            pltpu.SemaphoreType.DMA((3,)),
            pltpu.SemaphoreType.DMA((2, groups)),
            pltpu.SemaphoreType.DMA((2, rows)),
            pltpu.SemaphoreType.DMA((2, rows)),
        ],
        compiler_params=pltpu.CompilerParams(collective_id=1, has_side_effects=True),
        name="couple_and_solve",
    )(*operands)


def column_tables(width, group):
    pos = np.arange(width)
    part = pos // group % 2
    slot = pos // (2 * group) * group + pos % group
    first = slot == 0
    freq = np.where(first & (part == 1), width // 2, slot)
    shift = np.where(first, 0, part) * (math.pi / 2)
    fine = 32
    outer = (np.arange(width // fine) * fine)[:, None] * freq[None, :] % width * (full_turn / width)
    inner = np.arange(fine)[:, None] * freq[None, :] % width * (full_turn / width) + shift[None, :]
    turns = np.stack([f(a) for a in (outer, inner) for f in (np.cos, np.sin)])
    sign = np.where(first, 0.0, 1.0 - 2.0 * part).astype(np.float32)
    weight = np.where(first, 1.0, 2.0).astype(np.float32)
    return turns.astype(np.float32), freq, sign, weight


def on_device(za, zb, w_in, b_in, w_out, b_out, unmix, kern):
    slab, quarter, width = za.shape
    hidden_local = w_in.shape[3]
    chans = unmix.shape[0]
    half = chans // 2
    rows = lax.axis_size("rows")
    groups = lax.axis_size("chan")
    height = slab * rows
    block = width // groups
    mine = chans // groups
    lanes = 64
    freq_groups = width // lanes
    chan_groups = rows // freq_groups
    triple = mine // chan_groups

    col_turns, freq, sign, weight = column_tables(width, lanes // 2)

    zb_cols = zb.reshape(slab * quarter, groups, block).transpose(1, 0, 2)
    za_wide = jnp.pad(za.reshape(slab * quarter, width), ((0, 0), (2, 128 + 2)))
    za_cols = jnp.stack(
        [za_wide[:, block * i : block * i + block + 128] for i in range(groups)], axis=0
    )
    taps = 9
    w_in_parts = w_in.reshape(taps * half, hidden_local).T.reshape(
        2, hidden_local // 2, taps * half
    )
    w_out_parts = w_out.reshape(taps * hidden_local, chans).T.reshape(
        2, chans // 2, taps * hidden_local
    )
    za_got, zb_got, w_in_all, w_out_all, bias, *table = gather(
        za_cols, zb_cols, w_in_parts, w_out_parts, b_in[None, :], jnp.asarray(col_turns), rows, groups, 2
    )
    turn = freq * (full_turn / width)
    lane_rows = np.stack([sign, weight * (1.0 / (height * width)), np.cos(turn), np.sin(turn)])
    lane_rows = lane_rows.astype(np.float32).reshape(4, freq_groups, lanes).transpose(1, 0, 2)
    lane_rows = np.concatenate([lane_rows, lane_rows], axis=2)
    row_turn = np.arange(height) * (full_turn / height)
    turns = np.stack([np.cos(row_turn), np.sin(row_turn)]).astype(np.float32)

    blocks = []
    for row in range(slab):
        order = np.arange(rows) * slab + row
        angles = np.arange(height)[:, None] * order[None, :] % height * (full_turn / height)
        blocks.append((np.cos(angles), np.sin(angles)))
    ahead = [np.concatenate([c, t], axis=1) for c, t in blocks]
    ahead += [np.concatenate([-t, c], axis=1) for c, t in blocks]
    behind = [np.concatenate([c.T, -t.T], axis=1) for c, t in blocks]

    def fixed(pieces):
        values = np.concatenate(pieces, axis=0)
        high = values.astype(jnp.bfloat16)
        low = (values - high.astype(np.float64)).astype(jnp.bfloat16)
        return jnp.asarray(high), jnp.asarray(low)

    operands = (
        za_got,
        zb_got,
        w_in_all.reshape(groups, hidden_local, taps * half),
        w_out_all.reshape(groups, chans, taps * hidden_local),
        bias,
        b_out,
        unmix,
        *table,
        *fixed(ahead),
        *fixed(behind),
        kern,
        jnp.asarray(turns),
        jnp.asarray(lane_rows),
    )
    dims = (slab, half, quarter, hidden_local, groups, block, width, height)
    return whole(operands, dims, (rows, triple, lanes))


def solution(mesh):
    placed = (
        P("rows", "chan", None),
        P("rows", "chan", None),
        P(None, None, None, "chan"),
        P("chan"),
        P(None, None, "chan", None, None),
        P(),
        P(),
        P(),
    )
    return jax.shard_map(
        on_device, mesh=mesh, in_specs=placed, out_specs=P("rows", "chan", None), check_vma=False
    )
```

```python
import math

import jax
import jax.numpy as jnp
import numpy as np
from jax import lax
from jax.experimental import pallas as pl
from jax.experimental.pallas import tpu as pltpu
from jax.sharding import PartitionSpec as P

full_turn = 2.0 * math.pi
vmem = pl.BlockSpec(memory_space=pltpu.VMEM)
mesh_ids = pl.DeviceIdType.MESH


def split(values):
    high = values.astype(jnp.bfloat16)
    return high, (values - high.astype(jnp.float32)).astype(jnp.bfloat16)


def gather_kernel(rows, chans, halves_of, *refs):
    za_ref, zb_ref, win_ref, wout_ref, bias_ref, turn_ref = refs[:6]
    za_out, zb_out, win_out, wout_out, bias_out, high_out, low_out = refs[6:13]
    za_sems, zb_sems, w_sems, pass_sems, own_sem = refs[13:]
    me_row = lax.axis_index("rows")
    me_chan = lax.axis_index("chan")
    core = lax.rem(me_row, 2)
    side = lax.rem(me_row // 2, halves_of)
    ring = halves_of * chans
    spot = side * chans + me_chan
    partner = (me_row + 1 - 2 * core, me_chan)
    barrier = pltpu.get_barrier_semaphore()
    peers = [(dr, dc) for dr in (0, 1, 2) for dc in range(chans) if (dr, dc) != (1, 0)]
    steps = (1, ring - 1, 2 + core * (ring - 4))

    def place(dr, dc):
        return (lax.rem(me_row + dr + rows - 1, rows), lax.rem(me_chan + dc, chans))

    def around(step):
        there = lax.rem(spot + step, ring)
        return (me_row + (there // chans - side) * 2, lax.rem(there, chans))

    for step in steps:
        pl.semaphore_signal(
            barrier, inc=1, device_id=around(ring - step), device_id_type=mesh_ids
        )
    for dr, dc in peers:
        pl.semaphore_signal(barrier, inc=1, device_id=place(dr, dc), device_id_type=mesh_ids)
    own = [
        pltpu.make_async_copy(win_ref, win_out.at[me_chan], own_sem.at[0]),
        pltpu.make_async_copy(wout_ref, wout_out.at[me_chan], own_sem.at[1]),
        pltpu.make_async_copy(za_ref.at[me_chan], za_out.at[1, me_chan], own_sem.at[2]),
        pltpu.make_async_copy(zb_ref.at[me_chan], zb_out.at[me_chan], own_sem.at[3]),
        pltpu.make_async_copy(bias_ref, bias_out.at[me_chan], own_sem.at[4]),
    ]
    for one in own:
        one.start()
    pl.semaphore_wait(barrier, len(peers) + len(steps))
    first = []
    for idx, step in enumerate(steps):
        for kind, (source, target) in enumerate(((wout_ref, wout_out), (win_ref, win_out))):
            first.append(
                pltpu.make_async_remote_copy(
                    src_ref=source.at[core],
                    dst_ref=target.at[me_chan, core],
                    send_sem=w_sems.at[0, kind, idx],
                    recv_sem=w_sems.at[1, kind, idx],
                    device_id=around(step),
                    device_id_type=mesh_ids,
                )
            )
    copies = []
    for idx, (dr, dc) in enumerate(peers):
        there = place(dr, dc)
        copies.append(
            pltpu.make_async_remote_copy(
                src_ref=za_ref.at[there[1]],
                dst_ref=za_out.at[2 - dr, me_chan],
                send_sem=za_sems.at[0, idx],
                recv_sem=za_sems.at[1, idx],
                device_id=there,
                device_id_type=mesh_ids,
            )
        )
    for dc in range(1, chans):
        peer = lax.rem(me_chan + dc, chans)
        pairs = ((zb_ref.at[peer], zb_out), (bias_ref, bias_out))
        for kind, (source, target) in enumerate(pairs):
            copies.append(
                pltpu.make_async_remote_copy(
                    src_ref=source,
                    dst_ref=target.at[me_chan],
                    send_sem=zb_sems.at[0, kind, dc],
                    recv_sem=zb_sems.at[1, kind, dc],
                    device_id=(me_row, peer),
                    device_id_type=mesh_ids,
                )
            )
    for one in first:
        one.start()
    for one in copies:
        one.start()
    fine = turn_ref.shape[1]

    def fill(outer, carry):
        at = pl.ds(outer, 1)
        values = turn_ref[0, at, :] * turn_ref[2] - turn_ref[1, at, :] * turn_ref[3]
        high, low = split(values)
        here = pl.ds(pl.multiple_of(outer * fine, fine), fine)
        high_out[here, :] = high
        low_out[here, :] = low
        return carry

    lax.fori_loop(0, high_out.shape[0] // fine, fill, 0)
    passed = []
    for idx, step in enumerate(steps):
        origin = lax.rem(spot + ring - step, ring)
        quarter = lax.rem(origin, chans)
        for kind, target in enumerate((wout_out, win_out)):
            first[2 * idx + kind].wait_recv()
            one = pltpu.make_async_remote_copy(
                src_ref=target.at[quarter, core],
                dst_ref=target.at[quarter, core],
                send_sem=pass_sems.at[0, kind, idx],
                recv_sem=pass_sems.at[1, kind, idx],
                device_id=partner,
                device_id_type=mesh_ids,
            )
            one.start()
            passed.append(one)
    for one in own:
        one.wait()
    for one in copies:
        one.wait()
    for one in passed:
        one.wait()
    for one in first:
        one.wait_send()


def gather(za_cols, zb_cols, w_in, w_out, bias, turns, rows, chans, halves_of):
    def kernel(*refs):
        gather_kernel(rows, chans, halves_of, *refs)

    def several(lead, x):
        return jax.ShapeDtypeStruct(lead + x.shape, x.dtype)

    return pl.pallas_call(
        kernel,
        out_shape=(
            several((3,), za_cols),
            several((), zb_cols),
            several((chans,), w_in),
            several((chans,), w_out),
            several((chans,), bias),
            jax.ShapeDtypeStruct((turns.shape[2],) * 2, jnp.bfloat16),
            jax.ShapeDtypeStruct((turns.shape[2],) * 2, jnp.bfloat16),
        ),
        in_specs=[vmem] * 6,
        out_specs=(vmem,) * 7,
        scratch_shapes=[
            pltpu.SemaphoreType.DMA((2, 3 * chans)),
            pltpu.SemaphoreType.DMA((2, 2, chans)),
            pltpu.SemaphoreType.DMA((2, 2, 3)),
            pltpu.SemaphoreType.DMA((2, 2, 3)),
            pltpu.SemaphoreType.DMA((5,)),
        ],
        compiler_params=pltpu.CompilerParams(collective_id=0, has_side_effects=True),
        name="gather_inputs",
    )(za_cols, zb_cols, w_in, w_out, bias, turns)


def as_column(line):
    size = line.shape[1]
    down = lax.broadcasted_iota(jnp.int32, (size, size), 0)
    along = lax.broadcasted_iota(jnp.int32, (size, size), 1)
    return jnp.sum(jnp.where(down == along, line, 0.0), axis=1, keepdims=True)


def couple_kernel(dims, refs, plane_ref, latent_ref, taps_ref, hidden_ref):
    slab, half, quarter, hidden_local, groups, block, width, height = dims
    za_ref, zb_ref, win_ref, wout_ref, bias_ref, bout_ref, unmix_ref, out_ref = refs
    wide = za_ref.shape[3]
    first_row = lax.axis_index("rows") * slab - slab
    first_col = lax.axis_index("chan") * block - 1
    span = 3 * half
    for row in range(3 * slab):
        line = first_row + row
        held = (line >= 0) & (line < height)
        for part in range(groups):
            piece = za_ref[row // slab, part].astype(jnp.float32)
            piece = piece[row % slab * quarter : (row % slab + 1) * quarter]
            plane_ref[row, pl.ds(part * quarter, quarter), :] = jnp.where(held, piece, 0.0)
        plane = plane_ref[row]
        for off in range(3):
            moved = plane if off == 0 else pltpu.roll(plane, wide - off, 1)
            taps_ref[pl.ds(row * span + off * half, half), :] = moved.astype(jnp.bfloat16)
    cols = first_col + lax.broadcasted_iota(jnp.int32, (hidden_local, wide), 1)
    inside = (cols >= 0) & (cols < width)
    deep = 3 * hidden_local
    weights = []
    for part in range(groups):
        joint = jnp.concatenate([win_ref[part, i].astype(jnp.float32) for i in range(2)], axis=0)
        weights.append(joint.T.astype(jnp.bfloat16))
    biases = [as_column(bias_ref[part]) for part in range(groups)]
    out_bias = jnp.concatenate([as_column(bout_ref[pl.ds(i, 1), :]) for i in range(2)], axis=0)
    for row in range(2 * slab):
        line = first_row + row + 1
        keep = inside & (line >= 0) & (line < height)
        stack = taps_ref[pl.ds(row * span, 3 * span), :]
        for part in range(groups):
            value = lax.dot_general(
                weights[part], stack, (((1,), (0,)), ((), ())), preferred_element_type=jnp.float32
            )
            value = jnp.maximum(value + biases[part], 0.0)
            value = jnp.where(keep, value, 0.0)
            for off in range(3):
                moved = value if off == 0 else pltpu.roll(value, wide - off, 1)
                hidden_ref[part, pl.ds(row * deep + off * hidden_local, hidden_local), :] = moved[
                    :, :block
                ].astype(jnp.bfloat16)
    share = unmix_ref.shape[0] // groups
    for row in range(slab):
        raw = out_bias + jnp.zeros((2 * half, block), jnp.float32)
        for part in range(groups):
            raw = raw + jnp.dot(
                wout_ref[part],
                hidden_ref[part, pl.ds(row * deep, 3 * deep), :],
                preferred_element_type=jnp.float32,
            )
        for part in range(groups):
            piece = zb_ref[part].astype(jnp.float32)[row * quarter : (row + 1) * quarter]
            latent_ref[row, pl.ds(part * quarter, quarter), :] = piece
        latent = latent_ref[row]
        coupled = (latent - raw[half:]) * jnp.exp(-jnp.tanh(raw[:half]))
        own = pltpu.roll(plane_ref[slab + row], wide - 2, 1)[:, :block]
        joined = jnp.concatenate([own, coupled], axis=0)
        mixed = jnp.dot(
            unmix_ref[...],
            joined,
            precision=lax.Precision.HIGHEST,
            preferred_element_type=jnp.float32,
        )
        for part in range(groups):
            out_ref[part, pl.ds(row * share, share), :] = mixed[part * share : (part + 1) * share]


def outward(turn, count):
    return count // 2 + (turn + 1) // 2 * (1 - 2 * lax.rem(turn, 2))


def main_kernel(dims, counts, *refs):
    slab, half, quarter, hidden_local, groups, block, width, height = dims
    rows, triple, lanes = counts
    couple_refs = refs[:7]
    thigh_ref, tlow_ref, fhigh_ref, flow_ref, bhigh_ref, blow_ref = refs[7:13]
    kern_ref, turn_ref, lane_ref, out_ref = refs[13:17]
    plane_ref, latent_ref, taps_ref, hidden_ref, kern_cols = refs[17:22]
    mix_ref, mixed_ref, send_ref, got_ref, back_ref, home_ref = refs[22:28]
    work_ref, own_sem, chan_sem, there_sem, back_sem = refs[28:]
    mine = 2 * half // groups
    tile = 2 * lanes
    freq_groups = width // lanes
    chan_groups = rows // freq_groups
    me_row = lax.axis_index("rows")
    me_chan = lax.axis_index("chan")
    barrier = pltpu.get_barrier_semaphore()

    def greet(turn, carry):
        step = outward(turn, rows)
        pl.semaphore_signal(
            barrier,
            inc=1,
            device_id=(lax.rem(me_row + step, rows), me_chan),
            device_id_type=mesh_ids,
        )
        return carry

    for step in range(1, groups):
        pl.semaphore_signal(
            barrier,
            inc=1,
            device_id=(me_row, lax.rem(me_chan + step, groups)),
            device_id_type=mesh_ids,
        )
    lax.fori_loop(0, rows - 1, greet, 0)
    couple_kernel(
        dims, tuple(couple_refs) + (mix_ref,), plane_ref, latent_ref, taps_ref, hidden_ref
    )
    at = lax.broadcasted_iota(jnp.int32, kern_cols.shape, 1)
    spread = jnp.zeros(kern_cols.shape, jnp.float32)
    for row_off in range(3):
        for col_off in range(3):
            column = as_column(kern_ref[row_off, pl.ds(col_off, 1), :])
            spread = jnp.where(at == 3 * row_off + col_off, column, spread)
    kern_cols[...] = spread
    pl.semaphore_wait(barrier, rows - 1 + groups - 1)

    swaps = []
    for step in range(1, groups):
        peer = lax.rem(me_chan + step, groups)
        swaps.append(
            pltpu.make_async_remote_copy(
                src_ref=mix_ref.at[peer],
                dst_ref=mixed_ref.at[me_chan],
                send_sem=chan_sem.at[0, step],
                recv_sem=chan_sem.at[1, step],
                device_id=(me_row, peer),
                device_id_type=mesh_ids,
            )
        )
    for one in swaps:
        one.start()
    own = pltpu.make_async_copy(mix_ref.at[me_chan], mixed_ref.at[me_chan], own_sem.at[0])
    own.start()
    own.wait()
    for one in swaps:
        one.wait()

    high, low = split(jnp.concatenate([mixed_ref[i] for i in range(groups)], axis=1))
    lead = slab * mine
    both = jnp.dot(
        jnp.concatenate([high, low], axis=0), thigh_ref[...], preferred_element_type=jnp.float32
    )
    packed = both[:lead] + both[lead:]
    packed = packed + jnp.dot(high, tlow_ref[...], preferred_element_type=jnp.float32)
    lane = lax.broadcasted_iota(jnp.int32, (mine, tile), 1)
    for pair in range(freq_groups // 2):
        first = packed[:mine, pair * tile : (pair + 1) * tile]
        second = packed[mine:, pair * tile : (pair + 1) * tile]
        even = jnp.where(lane < lanes, first, pltpu.roll(second, lanes, 1))
        odd = jnp.where(lane < lanes, pltpu.roll(first, lanes, 1), second)
        for which, value in ((2 * pair, even), (2 * pair + 1, odd)):
            for group in range(chan_groups):
                send_ref[which * chan_groups + group] = value[
                    group * triple : (group + 1) * triple
                ]

    def exchange(source, target, sems, own_at):
        def copy(step):
            peer = lax.rem(me_row + step, rows)
            return pltpu.make_async_remote_copy(
                src_ref=source.at[peer],
                dst_ref=target.at[me_row],
                send_sem=sems.at[0, step],
                recv_sem=sems.at[1, step],
                device_id=(peer, me_chan),
                device_id_type=mesh_ids,
            )

        def start(turn, carry):
            copy(outward(turn, rows)).start()
            return carry

        def finish(step, carry):
            copy(step).wait()
            return carry

        lax.fori_loop(0, rows - 1, start, 0)
        kept = pltpu.make_async_copy(source.at[me_row], target.at[me_row], own_sem.at[own_at])
        kept.start()
        kept.wait()
        lax.fori_loop(1, rows, finish, 0)

    exchange(send_ref, got_ref, there_sem, 1)

    lane = lax.broadcasted_iota(jnp.int32, (rows, tile), 1)
    lane_table = lane_ref[me_row // chan_groups]
    sign = lane_table[0:1]
    scale = lane_table[1:2]
    cos_v = lane_table[2:3]
    sin_v = lane_table[3:4]
    chan_first = me_chan * mine + lax.rem(me_row, chan_groups) * triple
    stacks = []
    for chan in range(triple):
        data = got_ref[:, chan, :]
        other = jnp.where(
            lax.rem(lane, lanes) < lanes // 2,
            pltpu.roll(data, tile - lanes // 2, 1),
            pltpu.roll(data, lanes // 2, 1),
        )
        stacks.append(jnp.concatenate([data, other * sign], axis=0))
    high, low = split(jnp.concatenate(stacks, axis=1))
    forward = jnp.dot(fhigh_ref[...], high, preferred_element_type=jnp.float32)
    forward = forward + jnp.dot(fhigh_ref[...], low, preferred_element_type=jnp.float32)
    forward = forward + jnp.dot(flow_ref[...], high, preferred_element_type=jnp.float32)
    cos_u = as_column(turn_ref[pl.ds(0, 1), :])
    sin_u = as_column(turn_ref[pl.ds(1, 1), :])
    solved = []
    for chan in range(triple):
        piece = forward[:, chan * tile : (chan + 1) * tile]
        parts = [piece[i * height : (i + 1) * height] for i in range(4)]
        real_part = parts[0] + pltpu.roll(parts[1], lanes, 1)
        imag_part = parts[2] + pltpu.roll(parts[3], lanes, 1)
        stencil = kern_cols[pl.ds(chan_first + chan, 1), :]
        taps = [stencil[:, i : i + 1] for i in range(9)]
        near = [taps[3 * i + 1] + (taps[3 * i] + taps[3 * i + 2]) * cos_v for i in range(3)]
        near += [(taps[3 * i + 2] - taps[3 * i]) * sin_v for i in range(3)]
        symbol_real = near[1] + (near[0] + near[2]) * cos_u + (near[3] - near[5]) * sin_u
        symbol_imag = near[4] + (near[3] + near[5]) * cos_u + (near[2] - near[0]) * sin_u
        factor = scale / (symbol_real * symbol_real + symbol_imag * symbol_imag)
        solved.append(
            jnp.concatenate(
                [
                    (real_part * symbol_real + imag_part * symbol_imag) * factor,
                    (imag_part * symbol_real - real_part * symbol_imag) * factor,
                ],
                axis=0,
            )
        )
    high, low = split(jnp.concatenate(solved, axis=1))
    inverse = jnp.dot(bhigh_ref[...], high, preferred_element_type=jnp.float32)
    inverse = inverse + jnp.dot(bhigh_ref[...], low, preferred_element_type=jnp.float32)
    inverse = inverse + jnp.dot(blow_ref[...], high, preferred_element_type=jnp.float32)
    for chan in range(triple):
        piece = inverse[:, chan * tile : (chan + 1) * tile]
        back_ref[:, chan, :] = jnp.where(
            lane < lanes, piece[:rows], pltpu.roll(piece[rows:], lanes, 1)
        )

    exchange(back_ref, home_ref, back_sem, 2)

    for which in range(rows):
        work_ref[which // chan_groups, pl.ds(which % chan_groups * triple, triple), :] = home_ref[
            which
        ]
    lane = lax.broadcasted_iota(jnp.int32, (mine, tile), 1)
    upper = []
    lower = []
    for pair in range(freq_groups // 2):
        even = work_ref[2 * pair]
        odd = work_ref[2 * pair + 1]
        upper.append(jnp.where(lane < lanes, even, pltpu.roll(odd, lanes, 1)))
        lower.append(jnp.where(lane < lanes, pltpu.roll(even, lanes, 1), odd))
    final = jnp.concatenate(
        [jnp.concatenate(upper, axis=1), jnp.concatenate(lower, axis=1)], axis=0
    )
    high, low = split(final)

    def across(values, table):
        return lax.dot_general(
            values, table[...], (((1,), (1,)), ((), ())), preferred_element_type=jnp.float32
        )

    both = across(jnp.concatenate([high, low], axis=0), thigh_ref)
    result = both[:lead] + both[lead:] + across(high, tlow_ref)
    for row in range(slab):
        out_ref[row] = result[row * mine : (row + 1) * mine]


def whole(operands, dims, counts):
    slab, half, quarter, hidden_local, groups, block, width, height = dims
    rows, triple, lanes = counts
    wide = operands[0].shape[3]
    mine = 2 * half // groups
    tile = 2 * lanes

    def kernel(*refs):
        main_kernel(dims, counts, *refs)

    mix = pltpu.VMEM((groups, slab * mine, block), jnp.float32)
    message = pltpu.VMEM((rows, triple, tile), jnp.float32)
    return pl.pallas_call(
        kernel,
        out_shape=jax.ShapeDtypeStruct((slab, mine, width), jnp.float32),
        in_specs=[vmem] * len(operands),
        out_specs=vmem,
        scratch_shapes=[
            pltpu.VMEM((3 * slab, half, wide), jnp.float32),
            pltpu.VMEM((slab, half, block), jnp.float32),
            pltpu.VMEM((3 * slab * 3 * half, wide), jnp.bfloat16),
            pltpu.VMEM((groups, 2 * slab * 3 * hidden_local, block), jnp.bfloat16),
            pltpu.VMEM((2 * half, tile), jnp.float32),
            mix,
            mix,
            message,
            message,
            message,
            message,
            pltpu.VMEM((width // lanes, mine, tile), jnp.float32),
            pltpu.SemaphoreType.DMA((3,)),
            pltpu.SemaphoreType.DMA((2, groups)),
            pltpu.SemaphoreType.DMA((2, rows)),
            pltpu.SemaphoreType.DMA((2, rows)),
        ],
        compiler_params=pltpu.CompilerParams(collective_id=1, has_side_effects=True),
        name="couple_and_solve",
    )(*operands)


def column_tables(width, group):
    pos = np.arange(width)
    part = pos // group % 2
    slot = pos // (2 * group) * group + pos % group
    first = slot == 0
    freq = np.where(first & (part == 1), width // 2, slot)
    shift = np.where(first, 0, part) * (math.pi / 2)
    fine = 32
    outer = (np.arange(width // fine) * fine)[:, None] * freq[None, :] % width * (full_turn / width)
    inner = np.arange(fine)[:, None] * freq[None, :] % width * (full_turn / width) + shift[None, :]
    turns = np.stack([f(a) for a in (outer, inner) for f in (np.cos, np.sin)])
    sign = np.where(first, 0.0, 1.0 - 2.0 * part).astype(np.float32)
    weight = np.where(first, 1.0, 2.0).astype(np.float32)
    return turns.astype(np.float32), freq, sign, weight


def on_device(za, zb, w_in, b_in, w_out, b_out, unmix, kern):
    slab, quarter, width = za.shape
    hidden_local = w_in.shape[3]
    chans = unmix.shape[0]
    half = chans // 2
    rows = lax.axis_size("rows")
    groups = lax.axis_size("chan")
    height = slab * rows
    block = width // groups
    mine = chans // groups
    lanes = 64
    freq_groups = width // lanes
    chan_groups = rows // freq_groups
    triple = mine // chan_groups

    col_turns, freq, sign, weight = column_tables(width, lanes // 2)

    zb_cols = zb.reshape(slab * quarter, groups, block).transpose(1, 0, 2)
    za_wide = jnp.pad(za.reshape(slab * quarter, width), ((0, 0), (2, 128 + 2)))
    za_cols = jnp.stack(
        [za_wide[:, block * i : block * i + block + 128] for i in range(groups)], axis=0
    )
    taps = 9
    w_in_parts = w_in.reshape(2, taps * half // 2, hidden_local)
    w_out_parts = w_out.reshape(taps * hidden_local, chans).T.reshape(
        2, chans // 2, taps * hidden_local
    )
    za_got, zb_got, w_in_all, w_out_all, bias, *table = gather(
        za_cols, zb_cols, w_in_parts, w_out_parts, b_in[None, :], jnp.asarray(col_turns), rows, groups, 2
    )
    turn = freq * (full_turn / width)
    lane_rows = np.stack([sign, weight * (1.0 / (height * width)), np.cos(turn), np.sin(turn)])
    lane_rows = lane_rows.astype(np.float32).reshape(4, freq_groups, lanes).transpose(1, 0, 2)
    lane_rows = np.concatenate([lane_rows, lane_rows], axis=2)
    row_turn = np.arange(height) * (full_turn / height)
    turns = np.stack([np.cos(row_turn), np.sin(row_turn)]).astype(np.float32)

    blocks = []
    for row in range(slab):
        order = np.arange(rows) * slab + row
        angles = np.arange(height)[:, None] * order[None, :] % height * (full_turn / height)
        blocks.append((np.cos(angles), np.sin(angles)))
    ahead = [np.concatenate([c, t], axis=1) for c, t in blocks]
    ahead += [np.concatenate([-t, c], axis=1) for c, t in blocks]
    behind = [np.concatenate([c.T, -t.T], axis=1) for c, t in blocks]

    def fixed(pieces):
        values = np.concatenate(pieces, axis=0)
        high = values.astype(jnp.bfloat16)
        low = (values - high.astype(np.float64)).astype(jnp.bfloat16)
        return jnp.asarray(high), jnp.asarray(low)

    operands = (
        za_got,
        zb_got,
        w_in_all,
        w_out_all.reshape(groups, chans, taps * hidden_local),
        bias,
        b_out,
        unmix,
        *table,
        *fixed(ahead),
        *fixed(behind),
        kern,
        jnp.asarray(turns),
        jnp.asarray(lane_rows),
    )
    dims = (slab, half, quarter, hidden_local, groups, block, width, height)
    return whole(operands, dims, (rows, triple, lanes))


def solution(mesh):
    placed = (
        P("rows", "chan", None),
        P("rows", "chan", None),
        P(None, None, None, "chan"),
        P("chan"),
        P(None, None, "chan", None, None),
        P(),
        P(),
        P(),
    )
    return jax.shard_map(
        on_device, mesh=mesh, in_specs=placed, out_specs=P("rows", "chan", None), check_vma=False
    )
```

```python
import math

import jax
import jax.numpy as jnp
import numpy as np
from jax import lax
from jax.experimental import pallas as pl
from jax.experimental.pallas import tpu as pltpu
from jax.sharding import PartitionSpec as P

full_turn = 2.0 * math.pi
vmem = pl.BlockSpec(memory_space=pltpu.VMEM)
mesh_ids = pl.DeviceIdType.MESH


def split(values):
    high = values.astype(jnp.bfloat16)
    return high, (values - high.astype(jnp.float32)).astype(jnp.bfloat16)


def gather_kernel(rows, chans, halves_of, *refs):
    za_ref, zb_ref, win_ref, wout_ref, bias_ref, turn_ref = refs[:6]
    za_out, zb_out, win_out, wout_out, bias_out, high_out, low_out = refs[6:13]
    za_sems, zb_sems, w_sems, pass_sems, own_sem = refs[13:]
    me_row = lax.axis_index("rows")
    me_chan = lax.axis_index("chan")
    core = lax.rem(me_row, 2)
    side = lax.rem(me_row // 2, halves_of)
    ring = halves_of * chans
    spot = side * chans + me_chan
    partner = (me_row + 1 - 2 * core, me_chan)
    barrier = pltpu.get_barrier_semaphore()
    peers = [(dr, dc) for dr in (0, 1, 2) for dc in range(chans) if (dr, dc) != (1, 0)]
    steps = (1, ring - 1, 2 + core * (ring - 4))

    def place(dr, dc):
        return (lax.rem(me_row + dr + rows - 1, rows), lax.rem(me_chan + dc, chans))

    def around(step):
        there = lax.rem(spot + step, ring)
        return (me_row + (there // chans - side) * 2, lax.rem(there, chans))

    def zb_block(peer):
        block = zb_out.shape[3]
        return zb_ref.at[:, :, pl.ds(pl.multiple_of(peer * block, block), block)]

    for step in steps:
        pl.semaphore_signal(
            barrier, inc=1, device_id=around(ring - step), device_id_type=mesh_ids
        )
    for dr, dc in peers:
        pl.semaphore_signal(barrier, inc=1, device_id=place(dr, dc), device_id_type=mesh_ids)
    own = [
        pltpu.make_async_copy(win_ref, win_out.at[me_chan], own_sem.at[0]),
        pltpu.make_async_copy(wout_ref, wout_out.at[me_chan], own_sem.at[1]),
        pltpu.make_async_copy(za_ref.at[me_chan], za_out.at[1, me_chan], own_sem.at[2]),
        pltpu.make_async_copy(zb_block(me_chan), zb_out.at[me_chan], own_sem.at[3]),
        pltpu.make_async_copy(bias_ref, bias_out.at[me_chan], own_sem.at[4]),
    ]
    for one in own:
        one.start()
    pl.semaphore_wait(barrier, len(peers) + len(steps))
    first = []
    for idx, step in enumerate(steps):
        for kind, (source, target) in enumerate(((wout_ref, wout_out), (win_ref, win_out))):
            first.append(
                pltpu.make_async_remote_copy(
                    src_ref=source.at[core],
                    dst_ref=target.at[me_chan, core],
                    send_sem=w_sems.at[0, kind, idx],
                    recv_sem=w_sems.at[1, kind, idx],
                    device_id=around(step),
                    device_id_type=mesh_ids,
                )
            )
    copies = []
    for idx, (dr, dc) in enumerate(peers):
        there = place(dr, dc)
        copies.append(
            pltpu.make_async_remote_copy(
                src_ref=za_ref.at[there[1]],
                dst_ref=za_out.at[2 - dr, me_chan],
                send_sem=za_sems.at[0, idx],
                recv_sem=za_sems.at[1, idx],
                device_id=there,
                device_id_type=mesh_ids,
            )
        )
    for dc in range(1, chans):
        peer = lax.rem(me_chan + dc, chans)
        pairs = ((zb_block(peer), zb_out), (bias_ref, bias_out))
        for kind, (source, target) in enumerate(pairs):
            copies.append(
                pltpu.make_async_remote_copy(
                    src_ref=source,
                    dst_ref=target.at[me_chan],
                    send_sem=zb_sems.at[0, kind, dc],
                    recv_sem=zb_sems.at[1, kind, dc],
                    device_id=(me_row, peer),
                    device_id_type=mesh_ids,
                )
            )
    for one in first:
        one.start()
    for one in copies:
        one.start()
    fine = turn_ref.shape[1]

    def fill(outer, carry):
        at = pl.ds(outer, 1)
        values = turn_ref[0, at, :] * turn_ref[2] - turn_ref[1, at, :] * turn_ref[3]
        high, low = split(values)
        here = pl.ds(pl.multiple_of(outer * fine, fine), fine)
        high_out[here, :] = high
        low_out[here, :] = low
        return carry

    lax.fori_loop(0, high_out.shape[0] // fine, fill, 0)
    passed = []
    for idx, step in enumerate(steps):
        origin = lax.rem(spot + ring - step, ring)
        quarter = lax.rem(origin, chans)
        for kind, target in enumerate((wout_out, win_out)):
            first[2 * idx + kind].wait_recv()
            one = pltpu.make_async_remote_copy(
                src_ref=target.at[quarter, core],
                dst_ref=target.at[quarter, core],
                send_sem=pass_sems.at[0, kind, idx],
                recv_sem=pass_sems.at[1, kind, idx],
                device_id=partner,
                device_id_type=mesh_ids,
            )
            one.start()
            passed.append(one)
    for one in own:
        one.wait()
    for one in copies:
        one.wait()
    for one in passed:
        one.wait()
    for one in first:
        one.wait_send()


def gather(za_cols, zb_turned, w_in, w_out, bias, turns, rows, chans, halves_of):
    def kernel(*refs):
        gather_kernel(rows, chans, halves_of, *refs)

    def several(lead, x):
        return jax.ShapeDtypeStruct(lead + x.shape, x.dtype)

    return pl.pallas_call(
        kernel,
        out_shape=(
            several((3,), za_cols),
            jax.ShapeDtypeStruct(
                (chans,) + zb_turned.shape[:2] + (zb_turned.shape[2] // chans,), zb_turned.dtype
            ),
            several((chans,), w_in),
            several((chans,), w_out),
            several((chans,), bias),
            jax.ShapeDtypeStruct((turns.shape[2],) * 2, jnp.bfloat16),
            jax.ShapeDtypeStruct((turns.shape[2],) * 2, jnp.bfloat16),
        ),
        in_specs=[vmem] * 6,
        out_specs=(vmem,) * 7,
        scratch_shapes=[
            pltpu.SemaphoreType.DMA((2, 3 * chans)),
            pltpu.SemaphoreType.DMA((2, 2, chans)),
            pltpu.SemaphoreType.DMA((2, 2, 3)),
            pltpu.SemaphoreType.DMA((2, 2, 3)),
            pltpu.SemaphoreType.DMA((5,)),
        ],
        compiler_params=pltpu.CompilerParams(collective_id=0, has_side_effects=True),
        name="gather_inputs",
    )(za_cols, zb_turned, w_in, w_out, bias, turns)


def as_column(line):
    size = line.shape[1]
    down = lax.broadcasted_iota(jnp.int32, (size, size), 0)
    along = lax.broadcasted_iota(jnp.int32, (size, size), 1)
    return jnp.sum(jnp.where(down == along, line, 0.0), axis=1, keepdims=True)


def couple_kernel(dims, refs, plane_ref, latent_ref, taps_ref, hidden_ref):
    slab, half, quarter, hidden_local, groups, block, width, height = dims
    za_ref, zb_ref, win_ref, wout_ref, bias_ref, bout_ref, unmix_ref, out_ref = refs
    wide = za_ref.shape[3]
    first_row = lax.axis_index("rows") * slab - slab
    first_col = lax.axis_index("chan") * block - 1
    span = 3 * half
    for row in range(3 * slab):
        line = first_row + row
        held = (line >= 0) & (line < height)
        for part in range(groups):
            piece = za_ref[row // slab, part].astype(jnp.float32)
            piece = piece[row % slab * quarter : (row % slab + 1) * quarter]
            plane_ref[row, pl.ds(part * quarter, quarter), :] = jnp.where(held, piece, 0.0)
        plane = plane_ref[row]
        for off in range(3):
            moved = plane if off == 0 else pltpu.roll(plane, wide - off, 1)
            taps_ref[pl.ds(row * span + off * half, half), :] = moved.astype(jnp.bfloat16)
    cols = first_col + lax.broadcasted_iota(jnp.int32, (hidden_local, wide), 1)
    inside = (cols >= 0) & (cols < width)
    deep = 3 * hidden_local
    weights = []
    for part in range(groups):
        joint = jnp.concatenate([win_ref[part, i].astype(jnp.float32) for i in range(2)], axis=0)
        weights.append(joint.T.astype(jnp.bfloat16))
    biases = [as_column(bias_ref[part]) for part in range(groups)]
    out_bias = jnp.concatenate([as_column(bout_ref[pl.ds(i, 1), :]) for i in range(2)], axis=0)
    for row in range(2 * slab):
        line = first_row + row + 1
        keep = inside & (line >= 0) & (line < height)
        stack = taps_ref[pl.ds(row * span, 3 * span), :]
        for part in range(groups):
            value = lax.dot_general(
                weights[part], stack, (((1,), (0,)), ((), ())), preferred_element_type=jnp.float32
            )
            value = jnp.maximum(value + biases[part], 0.0)
            value = jnp.where(keep, value, 0.0)
            for off in range(3):
                moved = value if off == 0 else pltpu.roll(value, wide - off, 1)
                hidden_ref[part, pl.ds(row * deep + off * hidden_local, hidden_local), :] = moved[
                    :, :block
                ].astype(jnp.bfloat16)
    share = unmix_ref.shape[0] // groups
    for row in range(slab):
        raw = out_bias + jnp.zeros((2 * half, block), jnp.float32)
        for part in range(groups):
            raw = raw + jnp.dot(
                wout_ref[part],
                hidden_ref[part, pl.ds(row * deep, 3 * deep), :],
                preferred_element_type=jnp.float32,
            )
        for part in range(groups):
            piece = zb_ref[part].astype(jnp.float32)[:, row, :]
            latent_ref[row, pl.ds(part * quarter, quarter), :] = piece
        latent = latent_ref[row]
        coupled = (latent - raw[half:]) * jnp.exp(-jnp.tanh(raw[:half]))
        own = pltpu.roll(plane_ref[slab + row], wide - 2, 1)[:, :block]
        joined = jnp.concatenate([own, coupled], axis=0)
        mixed = jnp.dot(
            unmix_ref[...],
            joined,
            precision=lax.Precision.HIGHEST,
            preferred_element_type=jnp.float32,
        )
        for part in range(groups):
            out_ref[part, pl.ds(row * share, share), :] = mixed[part * share : (part + 1) * share]


def outward(turn, count):
    return count // 2 + (turn + 1) // 2 * (1 - 2 * lax.rem(turn, 2))


def main_kernel(dims, counts, *refs):
    slab, half, quarter, hidden_local, groups, block, width, height = dims
    rows, triple, lanes = counts
    couple_refs = refs[:7]
    thigh_ref, tlow_ref, fhigh_ref, flow_ref, bhigh_ref, blow_ref = refs[7:13]
    kern_ref, turn_ref, lane_ref, out_ref = refs[13:17]
    plane_ref, latent_ref, taps_ref, hidden_ref, kern_cols = refs[17:22]
    mix_ref, mixed_ref, send_ref, got_ref, back_ref, home_ref = refs[22:28]
    work_ref, own_sem, chan_sem, there_sem, back_sem = refs[28:]
    mine = 2 * half // groups
    tile = 2 * lanes
    freq_groups = width // lanes
    chan_groups = rows // freq_groups
    me_row = lax.axis_index("rows")
    me_chan = lax.axis_index("chan")
    barrier = pltpu.get_barrier_semaphore()

    def greet(turn, carry):
        step = outward(turn, rows)
        pl.semaphore_signal(
            barrier,
            inc=1,
            device_id=(lax.rem(me_row + step, rows), me_chan),
            device_id_type=mesh_ids,
        )
        return carry

    for step in range(1, groups):
        pl.semaphore_signal(
            barrier,
            inc=1,
            device_id=(me_row, lax.rem(me_chan + step, groups)),
            device_id_type=mesh_ids,
        )
    lax.fori_loop(0, rows - 1, greet, 0)
    couple_kernel(
        dims, tuple(couple_refs) + (mix_ref,), plane_ref, latent_ref, taps_ref, hidden_ref
    )
    at = lax.broadcasted_iota(jnp.int32, kern_cols.shape, 1)
    spread = jnp.zeros(kern_cols.shape, jnp.float32)
    for row_off in range(3):
        for col_off in range(3):
            column = as_column(kern_ref[row_off, pl.ds(col_off, 1), :])
            spread = jnp.where(at == 3 * row_off + col_off, column, spread)
    kern_cols[...] = spread
    pl.semaphore_wait(barrier, rows - 1 + groups - 1)

    swaps = []
    for step in range(1, groups):
        peer = lax.rem(me_chan + step, groups)
        swaps.append(
            pltpu.make_async_remote_copy(
                src_ref=mix_ref.at[peer],
                dst_ref=mixed_ref.at[me_chan],
                send_sem=chan_sem.at[0, step],
                recv_sem=chan_sem.at[1, step],
                device_id=(me_row, peer),
                device_id_type=mesh_ids,
            )
        )
    for one in swaps:
        one.start()
    own = pltpu.make_async_copy(mix_ref.at[me_chan], mixed_ref.at[me_chan], own_sem.at[0])
    own.start()
    own.wait()
    for one in swaps:
        one.wait()

    high, low = split(jnp.concatenate([mixed_ref[i] for i in range(groups)], axis=1))
    lead = slab * mine
    both = jnp.dot(
        jnp.concatenate([high, low], axis=0), thigh_ref[...], preferred_element_type=jnp.float32
    )
    packed = both[:lead] + both[lead:]
    packed = packed + jnp.dot(high, tlow_ref[...], preferred_element_type=jnp.float32)
    lane = lax.broadcasted_iota(jnp.int32, (mine, tile), 1)
    for pair in range(freq_groups // 2):
        first = packed[:mine, pair * tile : (pair + 1) * tile]
        second = packed[mine:, pair * tile : (pair + 1) * tile]
        even = jnp.where(lane < lanes, first, pltpu.roll(second, lanes, 1))
        odd = jnp.where(lane < lanes, pltpu.roll(first, lanes, 1), second)
        for which, value in ((2 * pair, even), (2 * pair + 1, odd)):
            for group in range(chan_groups):
                send_ref[which * chan_groups + group] = value[
                    group * triple : (group + 1) * triple
                ]

    def exchange(source, target, sems, own_at):
        def copy(step):
            peer = lax.rem(me_row + step, rows)
            return pltpu.make_async_remote_copy(
                src_ref=source.at[peer],
                dst_ref=target.at[me_row],
                send_sem=sems.at[0, step],
                recv_sem=sems.at[1, step],
                device_id=(peer, me_chan),
                device_id_type=mesh_ids,
            )

        def start(turn, carry):
            copy(outward(turn, rows)).start()
            return carry

        def finish(step, carry):
            copy(step).wait()
            return carry

        lax.fori_loop(0, rows - 1, start, 0)
        kept = pltpu.make_async_copy(source.at[me_row], target.at[me_row], own_sem.at[own_at])
        kept.start()
        kept.wait()
        lax.fori_loop(1, rows, finish, 0)

    exchange(send_ref, got_ref, there_sem, 1)

    lane = lax.broadcasted_iota(jnp.int32, (rows, tile), 1)
    lane_table = lane_ref[me_row // chan_groups]
    sign = lane_table[0:1]
    scale = lane_table[1:2]
    cos_v = lane_table[2:3]
    sin_v = lane_table[3:4]
    chan_first = me_chan * mine + lax.rem(me_row, chan_groups) * triple
    stacks = []
    for chan in range(triple):
        data = got_ref[:, chan, :]
        other = jnp.where(
            lax.rem(lane, lanes) < lanes // 2,
            pltpu.roll(data, tile - lanes // 2, 1),
            pltpu.roll(data, lanes // 2, 1),
        )
        stacks.append(jnp.concatenate([data, other * sign], axis=0))
    high, low = split(jnp.concatenate(stacks, axis=1))
    forward = jnp.dot(fhigh_ref[...], high, preferred_element_type=jnp.float32)
    forward = forward + jnp.dot(fhigh_ref[...], low, preferred_element_type=jnp.float32)
    forward = forward + jnp.dot(flow_ref[...], high, preferred_element_type=jnp.float32)
    cos_u = as_column(turn_ref[pl.ds(0, 1), :])
    sin_u = as_column(turn_ref[pl.ds(1, 1), :])
    solved = []
    for chan in range(triple):
        piece = forward[:, chan * tile : (chan + 1) * tile]
        parts = [piece[i * height : (i + 1) * height] for i in range(4)]
        real_part = parts[0] + pltpu.roll(parts[1], lanes, 1)
        imag_part = parts[2] + pltpu.roll(parts[3], lanes, 1)
        stencil = kern_cols[pl.ds(chan_first + chan, 1), :]
        taps = [stencil[:, i : i + 1] for i in range(9)]
        near = [taps[3 * i + 1] + (taps[3 * i] + taps[3 * i + 2]) * cos_v for i in range(3)]
        near += [(taps[3 * i + 2] - taps[3 * i]) * sin_v for i in range(3)]
        symbol_real = near[1] + (near[0] + near[2]) * cos_u + (near[3] - near[5]) * sin_u
        symbol_imag = near[4] + (near[3] + near[5]) * cos_u + (near[2] - near[0]) * sin_u
        factor = scale / (symbol_real * symbol_real + symbol_imag * symbol_imag)
        solved.append(
            jnp.concatenate(
                [
                    (real_part * symbol_real + imag_part * symbol_imag) * factor,
                    (imag_part * symbol_real - real_part * symbol_imag) * factor,
                ],
                axis=0,
            )
        )
    high, low = split(jnp.concatenate(solved, axis=1))
    inverse = jnp.dot(bhigh_ref[...], high, preferred_element_type=jnp.float32)
    inverse = inverse + jnp.dot(bhigh_ref[...], low, preferred_element_type=jnp.float32)
    inverse = inverse + jnp.dot(blow_ref[...], high, preferred_element_type=jnp.float32)
    for chan in range(triple):
        piece = inverse[:, chan * tile : (chan + 1) * tile]
        back_ref[:, chan, :] = jnp.where(
            lane < lanes, piece[:rows], pltpu.roll(piece[rows:], lanes, 1)
        )

    exchange(back_ref, home_ref, back_sem, 2)

    for which in range(rows):
        work_ref[which // chan_groups, pl.ds(which % chan_groups * triple, triple), :] = home_ref[
            which
        ]
    lane = lax.broadcasted_iota(jnp.int32, (mine, tile), 1)
    upper = []
    lower = []
    for pair in range(freq_groups // 2):
        even = work_ref[2 * pair]
        odd = work_ref[2 * pair + 1]
        upper.append(jnp.where(lane < lanes, even, pltpu.roll(odd, lanes, 1)))
        lower.append(jnp.where(lane < lanes, pltpu.roll(even, lanes, 1), odd))
    final = jnp.concatenate(
        [jnp.concatenate(upper, axis=1), jnp.concatenate(lower, axis=1)], axis=0
    )
    high, low = split(final)

    def across(values, table):
        return lax.dot_general(
            values, table[...], (((1,), (1,)), ((), ())), preferred_element_type=jnp.float32
        )

    both = across(jnp.concatenate([high, low], axis=0), thigh_ref)
    result = both[:lead] + both[lead:] + across(high, tlow_ref)
    for row in range(slab):
        out_ref[row] = result[row * mine : (row + 1) * mine]


def whole(operands, dims, counts):
    slab, half, quarter, hidden_local, groups, block, width, height = dims
    rows, triple, lanes = counts
    wide = operands[0].shape[3]
    mine = 2 * half // groups
    tile = 2 * lanes

    def kernel(*refs):
        main_kernel(dims, counts, *refs)

    mix = pltpu.VMEM((groups, slab * mine, block), jnp.float32)
    message = pltpu.VMEM((rows, triple, tile), jnp.float32)
    return pl.pallas_call(
        kernel,
        out_shape=jax.ShapeDtypeStruct((slab, mine, width), jnp.float32),
        in_specs=[vmem] * len(operands),
        out_specs=vmem,
        scratch_shapes=[
            pltpu.VMEM((3 * slab, half, wide), jnp.float32),
            pltpu.VMEM((slab, half, block), jnp.float32),
            pltpu.VMEM((3 * slab * 3 * half, wide), jnp.bfloat16),
            pltpu.VMEM((groups, 2 * slab * 3 * hidden_local, block), jnp.bfloat16),
            pltpu.VMEM((2 * half, tile), jnp.float32),
            mix,
            mix,
            message,
            message,
            message,
            message,
            pltpu.VMEM((width // lanes, mine, tile), jnp.float32),
            pltpu.SemaphoreType.DMA((3,)),
            pltpu.SemaphoreType.DMA((2, groups)),
            pltpu.SemaphoreType.DMA((2, rows)),
            pltpu.SemaphoreType.DMA((2, rows)),
        ],
        compiler_params=pltpu.CompilerParams(collective_id=1, has_side_effects=True),
        name="couple_and_solve",
    )(*operands)


def column_tables(width, group):
    pos = np.arange(width)
    part = pos // group % 2
    slot = pos // (2 * group) * group + pos % group
    first = slot == 0
    freq = np.where(first & (part == 1), width // 2, slot)
    shift = np.where(first, 0, part) * (math.pi / 2)
    fine = 32
    outer = (np.arange(width // fine) * fine)[:, None] * freq[None, :] % width * (full_turn / width)
    inner = np.arange(fine)[:, None] * freq[None, :] % width * (full_turn / width) + shift[None, :]
    turns = np.stack([f(a) for a in (outer, inner) for f in (np.cos, np.sin)])
    sign = np.where(first, 0.0, 1.0 - 2.0 * part).astype(np.float32)
    weight = np.where(first, 1.0, 2.0).astype(np.float32)
    return turns.astype(np.float32), freq, sign, weight


def on_device(za, zb, w_in, b_in, w_out, b_out, unmix, kern):
    slab, quarter, width = za.shape
    hidden_local = w_in.shape[3]
    chans = unmix.shape[0]
    half = chans // 2
    rows = lax.axis_size("rows")
    groups = lax.axis_size("chan")
    height = slab * rows
    block = width // groups
    mine = chans // groups
    lanes = 64
    freq_groups = width // lanes
    chan_groups = rows // freq_groups
    triple = mine // chan_groups

    col_turns, freq, sign, weight = column_tables(width, lanes // 2)

    zb_turned = zb.transpose(1, 0, 2)
    za_wide = jnp.pad(za.reshape(slab * quarter, width), ((0, 0), (2, 128 + 2)))
    za_cols = jnp.stack(
        [za_wide[:, block * i : block * i + block + 128] for i in range(groups)], axis=0
    )
    taps = 9
    w_in_parts = w_in.reshape(2, taps * half // 2, hidden_local)
    w_out_parts = w_out.reshape(taps * hidden_local, chans).T.reshape(
        2, chans // 2, taps * hidden_local
    )
    za_got, zb_got, w_in_all, w_out_all, bias, *table = gather(
        za_cols, zb_turned, w_in_parts, w_out_parts, b_in[None, :], jnp.asarray(col_turns), rows, groups, 2
    )
    turn = freq * (full_turn / width)
    lane_rows = np.stack([sign, weight * (1.0 / (height * width)), np.cos(turn), np.sin(turn)])
    lane_rows = lane_rows.astype(np.float32).reshape(4, freq_groups, lanes).transpose(1, 0, 2)
    lane_rows = np.concatenate([lane_rows, lane_rows], axis=2)
    row_turn = np.arange(height) * (full_turn / height)
    turns = np.stack([np.cos(row_turn), np.sin(row_turn)]).astype(np.float32)

    blocks = []
    for row in range(slab):
        order = np.arange(rows) * slab + row
        angles = np.arange(height)[:, None] * order[None, :] % height * (full_turn / height)
        blocks.append((np.cos(angles), np.sin(angles)))
    ahead = [np.concatenate([c, t], axis=1) for c, t in blocks]
    ahead += [np.concatenate([-t, c], axis=1) for c, t in blocks]
    behind = [np.concatenate([c.T, -t.T], axis=1) for c, t in blocks]

    def fixed(pieces):
        values = np.concatenate(pieces, axis=0)
        high = values.astype(jnp.bfloat16)
        low = (values - high.astype(np.float64)).astype(jnp.bfloat16)
        return jnp.asarray(high), jnp.asarray(low)

    operands = (
        za_got,
        zb_got,
        w_in_all,
        w_out_all.reshape(groups, chans, taps * hidden_local),
        bias,
        b_out,
        unmix,
        *table,
        *fixed(ahead),
        *fixed(behind),
        kern,
        jnp.asarray(turns),
        jnp.asarray(lane_rows),
    )
    dims = (slab, half, quarter, hidden_local, groups, block, width, height)
    return whole(operands, dims, (rows, triple, lanes))


def solution(mesh):
    placed = (
        P("rows", "chan", None),
        P("rows", "chan", None),
        P(None, None, None, "chan"),
        P("chan"),
        P(None, None, "chan", None, None),
        P(),
        P(),
        P(),
    )
    return jax.shard_map(
        on_device, mesh=mesh, in_specs=placed, out_specs=P("rows", "chan", None), check_vma=False
    )
```
